512 devices in a mesh: ctx: 32 (over z_hi, y, x), head: 16 (over z_lo, core).
Axes of the slice: x: 4, y: 4, z: 16 (z_hi: 2, z_lo: 8; z = z_hi * 8 + z_lo), core: 2. Of those that a mesh axis runs over, the one named last changes fastest.
Arguments:
- stream: bfloat16 [8192, 8192], P('ctx', 'head')
- norm_gain: float32 [8192], replicated, may hold values from 0.1 to 1.9
- tile_vals: bfloat16 [16, 96, 128, 128], P('head', 'ctx')
- tile_row: int32 [16, 96], P('head'), may hold values from 0 to 63, as said below
- tile_col: int32 [16, 96], P('head'), may hold values from 0 to 5, as said below
- kept_count: int32 [16], P('head'), may hold values from 32 to 96, as said below
Outputs:
- attended: bfloat16 [8192, 4096], P('ctx', 'head')
The draws below stay inside these ranges and needn't reach their ends.
Inputs may be any that keep to these rules, and one draw needn't show every extreme that they name: `tile_row`: for each reader, its first kept_count slots name distinct (row block, column block) pairs; the other slots are unused. For every head of a reader, some row block holds both that head's query tile and its key tile among the live slots. `tile_col`: column block within the reader's 6 blocks. `kept_count`: some reader has all 96 slots live.
All inputs are finite; a program needn't handle non-finite values.
Results may differ from the reference program's by a relative error of at most 0.04.
Values may be sent and summed in bfloat16 or wider, within the bound.
No kernel may reach another device: no remote copies, remote signals or barrier semaphores. Data moves between devices by JAX's collectives and lax.ppermute only.
A program may use at most 64 MiB of HBM per device.

```python
import math
import jax
import jax.numpy as jnp
from jax import lax

D = 8192
HD = 128
HEADS = 32
TOKENS = 8192
CAP = 96
N_HEAD = 16


def kept_lists(key):
    base = jax.random.fold_in(key, 11)
    row_blocks = D // HD
    heads_dev = HEADS // N_HEAD
    columns = 3 * heads_dev
    cells = row_blocks * columns
    lowest = max(CAP // 3, 2 * heads_dev)
    keys = jax.random.split(base, 3 * N_HEAD + 2)
    head_ids = jnp.arange(heads_dev, dtype=jnp.int32)

    def one_reader(first, second, third):
        planted = jax.random.randint(first, (heads_dev,), 0, row_blocks).astype(jnp.int32)
        pair_cells = jnp.concatenate([planted * columns + head_ids, planted * columns + heads_dev + head_ids])
        order = jax.random.permutation(second, jnp.arange(cells, dtype=jnp.int32))
        taken = jnp.any(order[:, None] == pair_cells[None, :], axis=1).astype(jnp.int32)
        rest = order[jnp.argsort(taken, stable=True)][:CAP - 2 * heads_dev]
        listed = jnp.concatenate([pair_cells, rest])
        front = jax.random.permutation(third, jnp.arange(lowest, dtype=jnp.int32))
        slots = jnp.concatenate([front, jnp.arange(lowest, CAP, dtype=jnp.int32)])
        listed = listed[slots]
        flags = (slots < 2 * heads_dev).astype(jnp.int32)
        return ((listed // columns).astype(jnp.int32), (listed % columns).astype(jnp.int32), flags, planted)
    rows, cols, flags, planted = jax.vmap(one_reader)(keys[:N_HEAD], keys[N_HEAD:2 * N_HEAD], keys[2 * N_HEAD:3 * N_HEAD])
    counts = jax.random.randint(keys[3 * N_HEAD], (N_HEAD,), lowest, CAP + 1)
    chosen = jax.random.randint(keys[3 * N_HEAD + 1], (), 0, N_HEAD)
    counts = jnp.where(jnp.arange(N_HEAD) == chosen, CAP, counts)
    return (rows, cols, counts.astype(jnp.int32))


def draw_tile_row(key, part):
    return kept_lists(key)[0]


def draw_tile_col(key, part):
    return kept_lists(key)[1]


def draw_kept_count(key, part):
    return kept_lists(key)[2]


def draw_tile_vals(key, part):
    first = jax.random.fold_in(jax.random.fold_in(key, 5), 0)
    shape = (N_HEAD, CAP, HD, HD)
    values = jax.random.normal(first, shape, jnp.float32) * 0.035
    return values.astype(jnp.bfloat16)


def draw_stream(key, part):
    first = jax.random.fold_in(jax.random.fold_in(key, 7), 0)
    noise = jax.random.normal(first, (TOKENS, D), jnp.float32)
    values = noise
    return jnp.clip(values, -6.0, 6.0).astype(jnp.bfloat16)


def setup_inputs(seed: int = 0) -> dict:
    arg_keys = jax.random.split(jax.random.key(seed), 7)
    stream = draw_stream(jax.random.fold_in(arg_keys[6], 71), 0)
    norm_gain = jnp.clip(1.0 + 0.18 * jax.random.normal(arg_keys[1], (D,), jnp.float32), 0.1, 1.9)
    tile_vals = draw_tile_vals(jax.random.fold_in(arg_keys[6], 71), 0)
    tile_row = draw_tile_row(jax.random.fold_in(arg_keys[6], 71), 0)
    tile_col = draw_tile_col(jax.random.fold_in(arg_keys[6], 71), 0)
    kept_count = draw_kept_count(jax.random.fold_in(arg_keys[6], 71), 0)
    return {"stream": stream, "norm_gain": norm_gain, "tile_vals": tile_vals, "tile_row": tile_row, "tile_col": tile_col, "kept_count": kept_count}


rope_base = 1000000.0

def rotate(values, cosines, sines):
    half = values.shape[-1] // 2
    first = values[..., :half]
    second = values[..., half:]
    return jnp.concatenate([first * cosines - second * sines, first * sines + second * cosines], axis=-1)

def reference(stream, norm_gain, tile_vals, tile_row, tile_col, kept_count):
    wide = stream.astype(jnp.float32)
    mean_sq = lax.optimization_barrier(jnp.mean(wide * wide, axis=1, keepdims=True))
    normed = (wide * lax.rsqrt(mean_sq + 1e-05) * norm_gain).astype(jnp.bfloat16)
    heads_dev = HEADS // N_HEAD
    columns = 3 * heads_dev
    blocks = normed.reshape(TOKENS, D // HD, HD)
    half = HD // 2
    freq = jnp.exp(-math.log(rope_base) * jnp.arange(half, dtype=jnp.float32) / half)
    positions = jnp.arange(TOKENS, dtype=jnp.float32)
    angles = positions[:, None] * freq[None, :]
    cosines = jnp.cos(angles)[:, None, :]
    sines = jnp.sin(angles)[:, None, :]
    qblock = math.gcd(TOKENS, 512)
    scale = 1.0 / math.sqrt(HD)

    def reader(index):
        rows = tile_row[index]
        cols = tile_col[index]
        count = kept_count[index]
        tiles = tile_vals[index]

        def add_tile(total, slot):
            picked = lax.dynamic_index_in_dim(blocks, rows[slot], 1, keepdims=False)
            product = jnp.dot(picked, tiles[slot], preferred_element_type=jnp.float32)
            live = (slot < count).astype(jnp.float32)
            return (total.at[:, cols[slot], :].add(live * product), None)
        start = jnp.zeros((TOKENS, columns, HD), jnp.float32)
        proj, unused = lax.scan(add_tile, start, jnp.arange(CAP, dtype=jnp.int32))
        queries = rotate(proj[:, :heads_dev], cosines, sines).astype(jnp.bfloat16)
        keys = rotate(proj[:, heads_dev:2 * heads_dev], cosines, sines).astype(jnp.bfloat16)
        values = proj[:, 2 * heads_dev:].astype(jnp.bfloat16)
        key_pos = jnp.arange(TOKENS, dtype=jnp.int32)

        def one_block(number):
            first = (number * qblock).astype(jnp.int32)
            qpart = lax.dynamic_slice_in_dim(queries, first, qblock, 0)
            qpos = first + jnp.arange(qblock, dtype=jnp.int32)
            scores = jnp.einsum('thd,shd->hts', qpart.astype(jnp.float32), keys.astype(jnp.float32)) * scale
            keep = key_pos[None, :] <= qpos[:, None]
            top = lax.optimization_barrier(jnp.max(jnp.where(keep[None], scores, -1e+30), axis=-1))
            expo = jnp.where(keep[None], jnp.exp(scores - top[..., None]), 0.0)
            total = lax.optimization_barrier(jnp.sum(expo, axis=-1))
            probs = expo.astype(jnp.bfloat16)
            mixed = jnp.einsum('hts,shd->thd', probs.astype(jnp.float32), values.astype(jnp.float32))
            return mixed / jnp.transpose(total)[:, :, None]
        outs = lax.map(one_block, jnp.arange(TOKENS // qblock, dtype=jnp.int32))
        return outs.reshape(TOKENS, heads_dev * HD).astype(jnp.bfloat16)
    every = lax.map(reader, jnp.arange(N_HEAD, dtype=jnp.int32))
    return jnp.transpose(every, (1, 0, 2)).reshape(TOKENS, HEADS * HD)
```

```python
import functools
import math

import jax
import jax.numpy as jnp
from jax import lax
from jax.experimental import pallas as pl
from jax.experimental.pallas import tpu as pltpu
from jax.sharding import Mesh
from jax.sharding import PartitionSpec as P

D = 8192
HD = 128
HEADS = 32
TOK = 256
ROWS = D // HD
COLS = 6
PLANE = ("y", "x")
CTX = ("zh", "y", "x")
HEAD = ("zl", "core")
NEG = -1e30

rope_base = 1000000.0


VM = pl.BlockSpec(memory_space=pltpu.VMEM)
SM = pl.BlockSpec(memory_space=pltpu.SMEM)


def params(mib):
    return pltpu.CompilerParams(vmem_limit_bytes=mib * 1024 * 1024)


def scatter_kernel(row_ref, col_ref, live_ref, tiles_ref, w_ref):
    def clear(i, c):
        w_ref[i] = jnp.zeros((HD, COLS * HD), jnp.bfloat16)
        return c

    lax.fori_loop(0, ROWS, clear, 0)
    slots = tiles_ref.shape[0]

    def put(s, c):
        @pl.when(live_ref[s] > 0)
        def _():
            at = pl.multiple_of(col_ref[s] * HD, HD)
            w_ref[row_ref[s], :, pl.ds(at, HD)] = tiles_ref[s]

        return c

    lax.fori_loop(0, slots, put, 0)


def scatter(rows, cols, live, tiles):
    return pl.pallas_call(
        scatter_kernel,
        out_shape=jax.ShapeDtypeStruct((ROWS, HD, COLS * HD), jnp.bfloat16),
        in_specs=[SM, SM, SM, VM],
        out_specs=VM,
        compiler_params=params(24),
        name="scatter_tiles",
    )(rows, cols, live, tiles)


def project_kernel(core_ref, mine_ref, other_ref, w_ref, gain_ref, cos_ref, sin_ref,
                   keep_ref, send_ref, acc_ref):
    core = core_ref[0]
    chunk = mine_ref.shape[2]
    per = chunk // HD

    def square(i, tot):
        for ref in (mine_ref, other_ref):
            for k in range(per):
                v = ref[i, :, k * HD:(k + 1) * HD].astype(jnp.float32)
                tot = tot + v * v
        return tot

    tot = lax.fori_loop(0, 8, square, jnp.zeros((TOK, HD), jnp.float32))
    r = lax.rsqrt(jnp.sum(tot, axis=1, keepdims=True) / D + 1e-05)
    acc_ref[...] = jnp.zeros_like(acc_ref)

    def step(i, c):
        part = None
        for ref, cc in ((mine_ref, core), (other_ref, 1 - core)):
            x = ref[i].astype(jnp.float32) * r * gain_ref[2 * i + cc]
            w = w_ref[pl.ds((2 * i + cc) * per, per)].reshape(chunk, COLS * HD)
            d = jnp.dot(x.astype(jnp.bfloat16), w, preferred_element_type=jnp.float32)
            part = d if part is None else part + d
        acc_ref[...] += part
        return c

    lax.fori_loop(0, 8, step, 0)
    cosines = cos_ref[...]
    sines = sin_ref[...]

    def rot(v):
        return v * cosines + pltpu.roll(v, HD // 2, 1) * sines

    for n, ref in ((0, keep_ref), (3, send_ref)):
        q = rot(acc_ref[:, n * HD:(n + 1) * HD]).astype(jnp.bfloat16)
        k = rot(acc_ref[:, (n + 1) * HD:(n + 2) * HD]).astype(jnp.bfloat16)
        v = acc_ref[:, (n + 2) * HD:(n + 3) * HD]
        for half in range(2):
            at = slice(half * HD, (half + 1) * HD)
            ref[half] = q[at]
            ref[2 + half] = k[at]
            ref[4 + half] = v[at].T.astype(jnp.bfloat16)


def project(core, mine, other, w, gain, cosines, sines):
    one = jax.ShapeDtypeStruct((6, HD, HD), jnp.bfloat16)
    return pl.pallas_call(
        project_kernel,
        out_shape=(one, one),
        in_specs=[SM] + [VM] * 6,
        out_specs=(VM, VM),
        scratch_shapes=[pltpu.VMEM((TOK, COLS * HD), jnp.float32)],
        compiler_params=params(32),
        name="project",
    )(core, mine, other, w, gain, cosines, sines)


def attend_kernel(ids_ref, q_ref, kv_ref, out_ref, m_ref, l_ref, acc_ref):
    first = ids_ref[0]
    row = ids_ref[1]
    col = ids_ref[2]
    scale = math.log2(math.e) / math.sqrt(HD)

    def one_query(n, c):
        xs = n // 2
        which = n % 2
        own = first + 4 * row + xs
        qid = jnp.where(which == 0, own, 31 - own)
        q = q_ref[xs, pl.ds(2 * which, 2)].reshape(TOK, HD)
        m_ref[...] = jnp.full_like(m_ref, NEG)
        l_ref[...] = jnp.zeros_like(l_ref)
        acc_ref[...] = jnp.zeros_like(acc_ref)

        def tile(ys, kw, diagonal):
            k = kv_ref[ys, pl.ds(4 * kw, 2)].reshape(TOK, HD)
            vt = jnp.concatenate([kv_ref[ys, 4 * kw + 2], kv_ref[ys, 4 * kw + 3]], axis=1)
            s = lax.dot_general(k, q, (((1,), (1,)), ((), ())), preferred_element_type=jnp.float32)
            if diagonal:
                kp = lax.broadcasted_iota(jnp.int32, s.shape, 0)
                qp = lax.broadcasted_iota(jnp.int32, s.shape, 1)
                s = jnp.where(kp <= qp, s, NEG)
            old = m_ref[...]
            new = jnp.maximum(old, jnp.max(s, axis=0, keepdims=True))
            p = jnp.exp2((s - new) * scale)
            fac = jnp.exp2((old - new) * scale)
            m_ref[...] = new
            l_ref[...] = l_ref[...] * fac + jnp.sum(p, axis=0, keepdims=True)
            acc_ref[...] = acc_ref[...] * fac + jnp.dot(
                vt, p.astype(jnp.bfloat16), preferred_element_type=jnp.float32
            )

        def one_key(j, c2):
            ys = j // 2
            kw = j % 2
            kown = first + 4 * ys + col
            kid = jnp.where(kw == 0, kown, 31 - kown)

            @pl.when(kid < qid)
            def _():
                tile(ys, kw, False)

            @pl.when(kid == qid)
            def _():
                tile(ys, kw, True)

            return c2

        lax.fori_loop(0, 8, one_key, 0)
        total = l_ref[...]
        some = total > 0
        safe = jnp.where(some, total, 1.0)
        lse = jnp.where(some, m_ref[...] * scale + jnp.log2(safe), NEG)
        at = pl.ds(pl.multiple_of(which * TOK, TOK), TOK)
        out_ref[xs, 0:HD, at] = (acc_ref[...] / safe).astype(jnp.bfloat16)
        hi = lse.astype(jnp.bfloat16).astype(jnp.float32)
        mid = (lse - hi).astype(jnp.bfloat16).astype(jnp.float32)
        low = lse - hi - mid
        r = lax.broadcasted_iota(jnp.int32, (16, TOK), 0)
        extra = jnp.where(r == 0, hi, jnp.where(r == 1, mid, jnp.where(r == 2, low, 0.0)))
        out_ref[xs, HD:HD + 16, at] = extra.astype(jnp.bfloat16)
        return c

    lax.fori_loop(0, 8, one_query, 0)


def attend(ids, q, kv):
    return pl.pallas_call(
        attend_kernel,
        out_shape=jax.ShapeDtypeStruct((4, HD + 16, 2 * TOK), jnp.bfloat16),
        in_specs=[SM, VM, VM],
        out_specs=VM,
        scratch_shapes=[
            pltpu.VMEM((1, TOK), jnp.float32),
            pltpu.VMEM((1, TOK), jnp.float32),
            pltpu.VMEM((HD, TOK), jnp.float32),
        ],
        compiler_params=params(16),
        name="attend",
    )(ids, q, kv)


def combine_kernel(parts_ref, own_ref, back_ref):
    lses = []
    for i in range(4):
        e = parts_ref[i, HD:HD + 16].astype(jnp.float32)
        lses.append(e[0:1] + e[1:2] + e[2:3])
    top = functools.reduce(jnp.maximum, lses)
    ws = [jnp.exp2(v - top) for v in lses]
    tot = ws[0] + ws[1] + ws[2] + ws[3]
    o = None
    for i in range(4):
        t = parts_ref[i, 0:HD].astype(jnp.float32) * (ws[i] / tot)
        o = t if o is None else o + t
    own_ref[...] = o[:, :TOK].T.astype(jnp.bfloat16)
    back_ref[...] = o[:, TOK:].T.astype(jnp.bfloat16)


def combine(parts):
    one = jax.ShapeDtypeStruct((TOK, HD), jnp.bfloat16)
    return pl.pallas_call(
        combine_kernel,
        out_shape=(one, one),
        in_specs=[VM],
        out_specs=(VM, VM),
        compiler_params=params(16),
        name="combine",
    )(parts)


def spread(x, axis, n):
    many = jnp.broadcast_to(x[None], (n,) + x.shape)
    return lax.all_to_all(many, axis, 0, 0, tiled=True)


def local(stream, norm_gain, tile_vals, tile_row, tile_col, kept_count):
    zh = lax.axis_index("zh")
    core = lax.axis_index("core")
    plane = lax.axis_index("y") * 4 + lax.axis_index("x")
    block = zh * 16 + plane
    mine = lax.all_gather(stream, "zl", axis=0, tiled=False)
    other = lax.ppermute(mine, "core", [(0, 1), (1, 0)])
    tv = tile_vals[0]
    far = lax.ppermute(tv, "zh", [(0, 1), (1, 0)])
    tiles = spread(jnp.concatenate([tv, far], axis=0), PLANE, 16)
    tiles = tiles.reshape(-1, HD, HD)
    slot = jnp.arange(96, dtype=jnp.int32).reshape(2, 16, 3)

    def order(v):
        v = jnp.where(zh == 0, v, v[::-1])
        return jnp.transpose(v, (1, 0, 2)).reshape(96)

    rows = order(tile_row[0].reshape(2, 16, 3))
    cols = order(tile_col[0].reshape(2, 16, 3))
    live = (order(slot) < kept_count[0]).astype(jnp.int32)
    cols = cols // 2 + 3 * (cols % 2 != zh).astype(jnp.int32)
    w = scatter(rows, cols, live, tiles)
    half = HD // 2
    freq = jnp.exp(-math.log(rope_base) * jnp.arange(half, dtype=jnp.float32) / half)
    qpos = block * TOK + jnp.arange(TOK, dtype=jnp.int32)
    angles = qpos.astype(jnp.float32)[:, None] * freq[None, :]
    c = jnp.cos(angles)
    s = jnp.sin(angles)
    cosines = jnp.concatenate([c, c], axis=1)
    sines = jnp.concatenate([-s, s], axis=1)
    gain = norm_gain.reshape(16, 1, 512)
    keep, send = project(core.reshape(1), mine, other, w, gain, cosines, sines)
    swap = [(h * 16 + b, (1 - h) * 16 + 15 - b) for h in range(2) for b in range(16)]
    recv = lax.ppermute(send, CTX, swap)
    q = spread(jnp.concatenate([keep[:2], recv[:2]], axis=0), "x", 4)
    kv = spread(jnp.concatenate([keep[2:], recv[2:]], axis=0), "y", 4)
    ids = jnp.stack([zh * 16, lax.axis_index("y"), lax.axis_index("x")]).astype(jnp.int32)
    parts = lax.all_to_all(attend(ids, q, kv), "x", 0, 0, tiled=True)
    own, back = combine(parts)
    got = lax.ppermute(back, CTX, swap)
    return jnp.where(
        zh == 0, jnp.concatenate([own, got], axis=1), jnp.concatenate([got, own], axis=1)
    )


def solution(mesh):
    wide = Mesh(mesh.devices.reshape(2, 4, 4, 8, 2), CTX + HEAD)
    return jax.shard_map(
        local,
        mesh=wide,
        in_specs=(
            P(CTX, HEAD),
            P(),
            P(HEAD, CTX, None, None),
            P(HEAD, None),
            P(HEAD, None),
            P(HEAD),
        ),
        out_specs=P(CTX, HEAD),
        check_vma=False,
    )
```

```python
import functools
import math

import jax
import jax.numpy as jnp
from jax import lax
from jax.experimental import pallas as pl
from jax.experimental.pallas import tpu as pltpu
from jax.sharding import Mesh
from jax.sharding import PartitionSpec as P

D = 8192
HD = 128
TOK = 256
ROWS = D // HD
COLS = 6
PLANE = ("y", "x")
CTX = ("zh",) + PLANE
HEAD = ("zl", "core")
NEG = -1e30

rope_base = 1000000.0


VM = pl.BlockSpec(memory_space=pltpu.VMEM)
SM = pl.BlockSpec(memory_space=pltpu.SMEM)


def params(mib):
    return pltpu.CompilerParams(vmem_limit_bytes=mib * 1024 * 1024)


def scatter_kernel(row_ref, col_ref, live_ref, near_ref, there_ref, w_ref):
    def clear(i, c):
        w_ref[i] = jnp.zeros((HD, COLS * HD), jnp.bfloat16)
        return c

    lax.fori_loop(0, ROWS, clear, 0)
    half = near_ref.shape[0]
    for n, ref in enumerate((near_ref, there_ref)):

        def put(s, c, n=n, ref=ref):
            slot = n * half + s

            @pl.when(live_ref[slot] > 0)
            def _():
                at = pl.multiple_of(col_ref[slot] * HD, HD)
                w_ref[row_ref[slot], :, pl.ds(at, HD)] = ref[s]

            return c

        lax.fori_loop(0, half, put, 0)


def scatter(rows, cols, live, near_tiles, there_tiles):
    return pl.pallas_call(
        scatter_kernel,
        out_shape=jax.ShapeDtypeStruct((ROWS, HD, COLS * HD), jnp.bfloat16),
        in_specs=[SM, SM, SM, VM, VM],
        out_specs=VM,
        compiler_params=params(4),
        name="scatter_tiles",
    )(rows, cols, live, near_tiles, there_tiles)


def project_kernel(core_ref, mine_ref, other_ref, w_ref, gain_ref, cos_ref, sin_ref,
                   q_ref, kv_ref, acc_ref):
    core = core_ref[0]
    chunk = mine_ref.shape[2]
    per = chunk // HD

    def square(i, tot):
        for ref in (mine_ref, other_ref):
            for k in range(per):
                v = ref[i, :, k * HD:(k + 1) * HD].astype(jnp.float32)
                tot = tot + v * v
        return tot

    tot = lax.fori_loop(0, 8, square, jnp.zeros((TOK, HD), jnp.float32))
    r = lax.rsqrt(jnp.sum(tot, axis=1, keepdims=True) / D + 1e-05)
    acc_ref[...] = jnp.zeros_like(acc_ref)

    def step(i, c):
        part = None
        for ref, cc in ((mine_ref, core), (other_ref, 1 - core)):
            x = ref[i].astype(jnp.float32) * r * gain_ref[2 * i + cc]
            w = w_ref[pl.ds((2 * i + cc) * per, per)].reshape(chunk, COLS * HD)
            d = jnp.dot(x.astype(jnp.bfloat16), w, preferred_element_type=jnp.float32)
            part = d if part is None else part + d
        acc_ref[...] += part
        return c

    lax.fori_loop(0, 8, step, 0)
    cosines = cos_ref[...]
    sines = sin_ref[...]

    def rot(v):
        return v * cosines + pltpu.roll(v, HD // 2, 1) * sines

    for h in range(2):
        q = rot(acc_ref[:, h * HD:(h + 1) * HD])
        k = rot(acc_ref[:, (2 + h) * HD:(3 + h) * HD]).astype(jnp.bfloat16)
        v = acc_ref[:, (4 + h) * HD:(5 + h) * HD]
        for half in range(2):
            at = slice(half * HD, (half + 1) * HD)
            qt = q[at].T.astype(jnp.bfloat16)
            for copy in range(4):
                q_ref[copy, 2 * h + half] = qt
            kv_ref[4 * h + half] = k[at]
            kv_ref[4 * h + 2 + half] = v[at].T.astype(jnp.bfloat16)


def project(core, mine, other, w, gain, cosines, sines):
    return pl.pallas_call(
        project_kernel,
        out_shape=(
            jax.ShapeDtypeStruct((4, 4, HD, HD), jnp.bfloat16),
            jax.ShapeDtypeStruct((8, HD, HD), jnp.bfloat16),
        ),
        in_specs=[SM] + [VM] * 6,
        out_specs=(VM, VM),
        scratch_shapes=[pltpu.VMEM((TOK, COLS * HD), jnp.float32)],
        compiler_params=params(10),
        name="project",
    )(core, mine, other, w, gain, cosines, sines)


SCALE = math.log2(math.e) / math.sqrt(HD)


def load_q(q_ref, n, h):
    return jnp.concatenate([q_ref[n, 2 * h], q_ref[n, 2 * h + 1]], axis=1)


def load_k(ref, h):
    return ref[2 * h * 2:2 * h * 2 + 2].reshape(TOK, HD)


def load_v(ref, h):
    return jnp.concatenate([ref[4 * h + 2], ref[4 * h + 3]], axis=1)


def near_kernel(ids_ref, q_ref, k0_ref, k1_ref, k2_ref, k3_ref, acc_ref, stat_ref):
    y = ids_ref[1]
    x = ids_ref[2]
    refs = (k0_ref, k1_ref, k2_ref, k3_ref)
    kids = [4 * lax.rem(y + 4 - k, 4) + x for k in range(4)]
    gap = lax.broadcasted_iota(jnp.int32, (TOK, TOK), 0) - lax.broadcasted_iota(
        jnp.int32, (TOK, TOK), 1
    )

    def one_source(n, c):
        qid = 4 * y + n
        for h in range(2):
            q = load_q(q_ref, n, h)
            ss = []
            for ref, kid in zip(refs, kids):
                s = jnp.dot(load_k(ref, h), q, preferred_element_type=jnp.float32)
                ss.append(jnp.where(gap <= (qid - kid) * TOK, s, NEG))
            top = functools.reduce(jnp.maximum, [jnp.max(s, axis=0, keepdims=True) for s in ss])
            acc = None
            total = None
            for ref, kid, s in zip(refs, kids, ss):
                p = jnp.where(gap <= (qid - kid) * TOK, jnp.exp2((s - top) * SCALE), 0.0)
                t = jnp.sum(p, axis=0, keepdims=True)
                o = jnp.dot(
                    load_v(ref, h), p.astype(jnp.bfloat16), preferred_element_type=jnp.float32
                )
                acc = o if acc is None else acc + o
                total = t if total is None else total + t
            acc_ref[2 * n + h] = acc
            stat_ref[2 * n + h, 0:1] = top
            stat_ref[2 * n + h, 1:2] = total
        return c

    lax.fori_loop(0, 4, one_source, 0)


STATE = (
    jax.ShapeDtypeStruct((8, HD, TOK), jnp.float32),
    jax.ShapeDtypeStruct((8, 8, TOK), jnp.float32),
)


def near(ids, q, keys):
    return pl.pallas_call(
        near_kernel,
        out_shape=STATE,
        in_specs=[SM] + [VM] * 5,
        out_specs=(VM, VM),
        compiler_params=params(10),
        name="attend_near",
    )(ids, q, *keys)


def fold(q_ref, refs, n, h, acc, old, total):
    q = load_q(q_ref, n, h)
    ss = [jnp.dot(load_k(ref, h), q, preferred_element_type=jnp.float32) for ref in refs]
    top = functools.reduce(jnp.maximum, [jnp.max(s, axis=0, keepdims=True) for s in ss], old)
    fac = jnp.exp2((old - top) * SCALE)
    acc = acc * fac
    total = total * fac
    for s, ref in zip(ss, refs):
        p = jnp.exp2((s - top) * SCALE)
        total = total + jnp.sum(p, axis=0, keepdims=True)
        acc = acc + jnp.dot(
            load_v(ref, h), p.astype(jnp.bfloat16), preferred_element_type=jnp.float32
        )
    return acc, top, total


def far_kernel(ids_ref, q_ref, k0_ref, k1_ref, acc_in, stat_in, acc_ref, stat_ref):
    late = ids_ref[0] > 0

    def one_source(n, c):
        for h in range(2):
            i = 2 * n + h
            acc = acc_in[i]
            top = stat_in[i, 0:1]
            total = stat_in[i, 1:2]
            acc, top, total = fold(q_ref, (k0_ref, k1_ref), n, h, acc, top, total)
            acc_ref[i] = acc
            stat_ref[i, 0:1] = top
            stat_ref[i, 1:2] = total
        return c

    @pl.when(late)
    def _():
        lax.fori_loop(0, 4, one_source, 0)

    @pl.when(jnp.logical_not(late))
    def _():
        acc_ref[...] = acc_in[...]
        stat_ref[...] = stat_in[...]


def far(ids, q, fars, acc, stat):
    return pl.pallas_call(
        far_kernel,
        out_shape=STATE,
        in_specs=[SM] + [VM] * 5,
        out_specs=(VM, VM),
        compiler_params=params(10),
        name="attend_far",
    )(ids, q, *fars, acc, stat)


def last_kernel(ids_ref, q_ref, k0_ref, k1_ref, acc_ref, stat_ref, out_ref):
    late = ids_ref[0] > 0

    def finish(n, h, acc, top, total):
        some = total > 0
        safe = jnp.where(some, total, 1.0)
        lse = jnp.where(some, top * SCALE + jnp.log2(safe), NEG)
        at = slice(h * TOK, (h + 1) * TOK)
        out_ref[n, 0:HD, at] = (acc / safe).astype(jnp.bfloat16)
        hi = lse.astype(jnp.bfloat16).astype(jnp.float32)
        mid = (lse - hi).astype(jnp.bfloat16).astype(jnp.float32)
        low = lse - hi - mid
        r = lax.broadcasted_iota(jnp.int32, (16, TOK), 0)
        extra = jnp.where(r == 0, hi, jnp.where(r == 1, mid, jnp.where(r == 2, low, 0.0)))
        out_ref[n, HD:HD + 16, at] = extra.astype(jnp.bfloat16)

    def state(n, h):
        i = 2 * n + h
        return acc_ref[i], stat_ref[i, 0:1], stat_ref[i, 1:2]

    @pl.when(jnp.logical_not(late))
    def _():
        def one_source(n, c):
            for h in range(2):
                finish(n, h, *state(n, h))
            return c

        lax.fori_loop(0, 4, one_source, 0)

    @pl.when(late)
    def _():
        def one_source(n, c):
            for h in range(2):
                finish(n, h, *fold(q_ref, (k0_ref, k1_ref), n, h, *state(n, h)))
            return c

        lax.fori_loop(0, 4, one_source, 0)


def last(ids, q, fars, acc, stat):
    return pl.pallas_call(
        last_kernel,
        out_shape=jax.ShapeDtypeStruct((4, HD + 16, 2 * TOK), jnp.bfloat16),
        in_specs=[SM] + [VM] * 5,
        out_specs=VM,
        compiler_params=params(10),
        name="attend_last",
    )(ids, q, *fars, acc, stat)


def combine_kernel(parts_ref, out_ref):
    count = parts_ref.shape[0]
    lses = []
    for i in range(count):
        e = parts_ref[i, HD:HD + 16].astype(jnp.float32)
        lses.append(e[0:1] + e[1:2] + e[2:3])
    top = functools.reduce(jnp.maximum, lses)
    ws = [jnp.exp2(v - top) for v in lses]
    tot = sum(ws)
    o = None
    for i in range(count):
        t = parts_ref[i, 0:HD].astype(jnp.float32) * (ws[i] / tot)
        o = t if o is None else o + t
    out_ref[:, :HD] = o[:, :TOK].T.astype(jnp.bfloat16)
    out_ref[:, HD:] = o[:, TOK:].T.astype(jnp.bfloat16)


def combine(parts):
    return pl.pallas_call(
        combine_kernel,
        out_shape=jax.ShapeDtypeStruct((TOK, 2 * HD), jnp.bfloat16),
        in_specs=[VM],
        out_specs=VM,
        compiler_params=params(10),
        name="combine",
    )(parts)


def spread(x, axis, n):
    many = jnp.broadcast_to(x[None], (n,) + x.shape)
    return lax.all_to_all(many, axis, 0, 0, tiled=True)


def body(stream, norm_gain, tile_vals, tile_row, tile_col, kept_count):
    zh = lax.axis_index("zh")
    core = lax.axis_index("core")
    plane = lax.axis_index(PLANE)
    block = zh * 16 + plane
    mine = lax.all_gather(stream, "zl", axis=0, tiled=False)
    tv = tile_vals[0]
    there = lax.ppermute(tv, "zh", [(0, 1), (1, 0)])
    near_tiles = spread(tv, PLANE, 16).reshape(-1, HD, HD)
    there_tiles = spread(there, PLANE, 16).reshape(-1, HD, HD)

    def order(v):
        v = v.reshape(2, 48)
        return jnp.where(zh == 0, v, v[::-1]).reshape(96)

    rows = order(tile_row[0])
    cols = order(tile_col[0])
    slot = order(jnp.arange(96, dtype=jnp.int32))
    live = (slot < kept_count[0]).astype(jnp.int32)
    half = HD // 2
    freq = jnp.exp(-math.log(rope_base) * jnp.arange(half, dtype=jnp.float32) / half)
    qpos = block * TOK + jnp.arange(TOK, dtype=jnp.int32)
    angles = qpos.astype(jnp.float32)[:, None] * freq[None, :]
    c = jnp.cos(angles)
    s = jnp.sin(angles)
    cosines = jnp.concatenate([c, c], axis=1)
    sines = jnp.concatenate([-s, s], axis=1)
    gain = norm_gain.reshape(16, 1, 512)
    mine, near_tiles, there_tiles, rows, cols, live, gain, cosines, sines = (
        lax.optimization_barrier(
            (mine, near_tiles, there_tiles, rows, cols, live, gain, cosines, sines)
        )
    )
    other = lax.ppermute(mine, "core", [(0, 1), (1, 0)])
    w = scatter(rows, cols, live, near_tiles, there_tiles)
    q, kv = project(core.reshape(1), mine, other, w, gain, cosines, sines)
    fars = []
    for k in range(4):
        pairs = [
            (4 * y + x, 16 + 4 * ((y + k) % 4) + x) for y in range(4) for x in range(4)
        ]
        fars.append(lax.ppermute(kv, CTX, pairs))
    keys = [kv]
    for k in range(1, 4):
        keys.append(lax.ppermute(kv, "y", [(y, y + k) for y in range(4 - k)]))
    q = lax.all_to_all(q, "x", 0, 0, tiled=True)
    ids = jnp.stack([zh, lax.axis_index("y"), lax.axis_index("x")]).astype(jnp.int32)
    acc, stat = near(ids, q, keys)
    acc, stat = far(ids, q, fars[:2], acc, stat)
    parts = lax.all_to_all(last(ids, q, fars[2:], acc, stat), "x", 0, 0, tiled=True)
    return combine(parts)


def solution(mesh):
    wide = Mesh(mesh.devices.reshape(2, 4, 4, 8, 2), CTX + HEAD)
    return jax.shard_map(
        body,
        mesh=wide,
        in_specs=(
            P(CTX, HEAD),
            P(),
            P(HEAD, CTX, None, None),
            P(HEAD, None),
            P(HEAD, None),
            P(HEAD),
        ),
        out_specs=P(CTX, HEAD),
        check_vma=False,
    )
```

```python
import functools
import math

import jax
import jax.numpy as jnp
from jax import lax
from jax.experimental import pallas as pl
from jax.experimental.pallas import tpu as pltpu
from jax.sharding import Mesh
from jax.sharding import PartitionSpec as P

D = 8192
HD = 128
TOK = 256
ROWS = D // HD
COLS = 6
PLANE = ("y", "x")
CTX = ("zh",) + PLANE
HEAD = ("zl", "core")
NEG = -1e30

rope_base = 1000000.0


VM = pl.BlockSpec(memory_space=pltpu.VMEM)
SM = pl.BlockSpec(memory_space=pltpu.SMEM)


def params(mib):
    return pltpu.CompilerParams(vmem_limit_bytes=mib * 1024 * 1024)


def scatter_kernel(row_ref, col_ref, live_ref, near_ref, there_ref, w_ref):
    def clear(i, c):
        w_ref[i] = jnp.zeros((HD, COLS * HD), jnp.bfloat16)
        return c

    lax.fori_loop(0, ROWS, clear, 0)
    half = near_ref.shape[0]
    for n, ref in enumerate((near_ref, there_ref)):

        def put(s, c, n=n, ref=ref):
            slot = n * half + s

            @pl.when(live_ref[slot] > 0)
            def _():
                at = pl.multiple_of(col_ref[slot] * HD, HD)
                w_ref[row_ref[slot], :, pl.ds(at, HD)] = ref[s]

            return c

        lax.fori_loop(0, half, put, 0)


def scatter(rows, cols, live, near_tiles, there_tiles):
    return pl.pallas_call(
        scatter_kernel,
        out_shape=jax.ShapeDtypeStruct((ROWS, HD, COLS * HD), jnp.bfloat16),
        in_specs=[SM, SM, SM, VM, VM],
        out_specs=VM,
        compiler_params=params(4),
        name="scatter_tiles",
    )(rows, cols, live, near_tiles, there_tiles)


def project_kernel(core_ref, mine_ref, other_ref, w_ref, gain_ref, cos_ref, sin_ref,
                   q_ref, kv_ref, kv0_ref, kv1_ref, acc_ref):
    core = core_ref[0]
    chunk = mine_ref.shape[2]
    per = chunk // HD

    def square(i, tot):
        for ref in (mine_ref, other_ref):
            for k in range(per):
                v = ref[i, :, k * HD:(k + 1) * HD].astype(jnp.float32)
                tot = tot + v * v
        return tot

    tot = lax.fori_loop(0, 8, square, jnp.zeros((TOK, HD), jnp.float32))
    r = lax.rsqrt(jnp.sum(tot, axis=1, keepdims=True) / D + 1e-05)
    acc_ref[...] = jnp.zeros_like(acc_ref)

    def step(i, c):
        part = None
        for ref, cc in ((mine_ref, core), (other_ref, 1 - core)):
            x = ref[i].astype(jnp.float32) * r * gain_ref[2 * i + cc]
            w = w_ref[pl.ds((2 * i + cc) * per, per)].reshape(chunk, COLS * HD)
            d = jnp.dot(x.astype(jnp.bfloat16), w, preferred_element_type=jnp.float32)
            part = d if part is None else part + d
        acc_ref[...] += part
        return c

    lax.fori_loop(0, 8, step, 0)
    cosines = cos_ref[...]
    sines = sin_ref[...]

    def rot(v):
        return v * cosines + pltpu.roll(v, HD // 2, 1) * sines

    for h in range(2):
        q = rot(acc_ref[:, h * HD:(h + 1) * HD])
        k = rot(acc_ref[:, (2 + h) * HD:(3 + h) * HD]).astype(jnp.bfloat16)
        v = acc_ref[:, (4 + h) * HD:(5 + h) * HD]
        for half in range(2):
            at = slice(half * HD, (half + 1) * HD)
            qt = q[at].T.astype(jnp.bfloat16)
            for copy in range(4):
                q_ref[copy, 2 * h + half] = qt
            vt = v[at].T.astype(jnp.bfloat16)
            one = (kv0_ref, kv1_ref)[h]
            kv_ref[4 * h + half] = k[at]
            kv_ref[4 * h + 2 + half] = vt
            one[half] = k[at]
            one[2 + half] = vt


def project(core, mine, other, w, gain, cosines, sines):
    return pl.pallas_call(
        project_kernel,
        out_shape=(
            jax.ShapeDtypeStruct((4, 4, HD, HD), jnp.bfloat16),
            jax.ShapeDtypeStruct((8, HD, HD), jnp.bfloat16),
            jax.ShapeDtypeStruct((4, HD, HD), jnp.bfloat16),
            jax.ShapeDtypeStruct((4, HD, HD), jnp.bfloat16),
        ),
        in_specs=[SM] + [VM] * 6,
        out_specs=(VM,) * 4,
        scratch_shapes=[pltpu.VMEM((TOK, COLS * HD), jnp.float32)],
        compiler_params=params(10),
        name="project",
    )(core, mine, other, w, gain, cosines, sines)


SCALE = math.log2(math.e) / math.sqrt(HD)


def load_q(q_ref, n, h):
    return jnp.concatenate([q_ref[n, 2 * h], q_ref[n, 2 * h + 1]], axis=1)


def load_k(ref, h):
    return ref[2 * h * 2:2 * h * 2 + 2].reshape(TOK, HD)


def load_v(ref, h):
    return jnp.concatenate([ref[4 * h + 2], ref[4 * h + 3]], axis=1)


def near_kernel(ids_ref, q_ref, k0_ref, k1_ref, k2_ref, k3_ref, acc_ref, stat_ref):
    y = ids_ref[1]
    x = ids_ref[2]
    refs = (k0_ref, k1_ref, k2_ref, k3_ref)
    kids = [4 * lax.rem(y + 4 - k, 4) + x for k in range(4)]
    gap = lax.broadcasted_iota(jnp.int32, (TOK, TOK), 0) - lax.broadcasted_iota(
        jnp.int32, (TOK, TOK), 1
    )

    def one_source(n, c):
        qid = 4 * y + n
        for h in range(2):
            q = load_q(q_ref, n, h)
            ss = []
            for ref, kid in zip(refs, kids):
                s = jnp.dot(load_k(ref, h), q, preferred_element_type=jnp.float32)
                ss.append(jnp.where(gap <= (qid - kid) * TOK, s, NEG))
            top = functools.reduce(jnp.maximum, [jnp.max(s, axis=0, keepdims=True) for s in ss])
            acc = None
            total = None
            for ref, kid, s in zip(refs, kids, ss):
                p = jnp.where(gap <= (qid - kid) * TOK, jnp.exp2((s - top) * SCALE), 0.0)
                t = jnp.sum(p, axis=0, keepdims=True)
                o = jnp.dot(
                    load_v(ref, h), p.astype(jnp.bfloat16), preferred_element_type=jnp.float32
                )
                acc = o if acc is None else acc + o
                total = t if total is None else total + t
            acc_ref[2 * n + h] = acc
            stat_ref[2 * n + h, 0:1] = top
            stat_ref[2 * n + h, 1:2] = total
        return c

    lax.fori_loop(0, 4, one_source, 0)


STATE = (
    jax.ShapeDtypeStruct((8, HD, TOK), jnp.float32),
    jax.ShapeDtypeStruct((8, 8, TOK), jnp.float32),
)


def near(ids, q, keys):
    return pl.pallas_call(
        near_kernel,
        out_shape=STATE,
        in_specs=[SM] + [VM] * 5,
        out_specs=(VM, VM),
        compiler_params=params(10),
        name="attend_near",
    )(ids, q, *keys)


def fold(q_ref, refs, n, h, acc, old, total):
    q = load_q(q_ref, n, h)
    ss = [jnp.dot(load_k(ref, 0), q, preferred_element_type=jnp.float32) for ref in refs]
    top = functools.reduce(jnp.maximum, [jnp.max(s, axis=0, keepdims=True) for s in ss], old)
    fac = jnp.exp2((old - top) * SCALE)
    acc = acc * fac
    total = total * fac
    for s, ref in zip(ss, refs):
        p = jnp.exp2((s - top) * SCALE)
        total = total + jnp.sum(p, axis=0, keepdims=True)
        acc = acc + jnp.dot(
            load_v(ref, 0), p.astype(jnp.bfloat16), preferred_element_type=jnp.float32
        )
    return acc, top, total


def far_kernel(head, ids_ref, q_ref, kv_ref, acc_ref, stat_ref, *rest):
    out_ref = rest[-1]
    late = ids_ref[0] > 0

    def finish(n, acc, top, total):
        some = total > 0
        safe = jnp.where(some, total, 1.0)
        lse = jnp.where(some, top * SCALE + jnp.log2(safe), NEG)
        out_ref[n, head, 0:HD] = (acc / safe).astype(jnp.bfloat16)
        hi = lse.astype(jnp.bfloat16).astype(jnp.float32)
        mid = (lse - hi).astype(jnp.bfloat16).astype(jnp.float32)
        low = lse - hi - mid
        r = lax.broadcasted_iota(jnp.int32, (16, TOK), 0)
        extra = jnp.where(r == 0, hi, jnp.where(r == 1, mid, jnp.where(r == 2, low, 0.0)))
        out_ref[n, head, HD:HD + 16] = extra.astype(jnp.bfloat16)

    def state(n):
        i = 2 * n + head
        return acc_ref[i], stat_ref[i, 0:1], stat_ref[i, 1:2]

    @pl.when(jnp.logical_not(late))
    def _():
        for n in range(4):
            finish(n, *state(n))

    @pl.when(late)
    def _():
        def one_source(m, c):
            for n in (2 * m, 2 * m + 1):
                finish(n, *fold(q_ref, [kv_ref.at[k] for k in range(4)], n, head, *state(n)))
            return c

        lax.fori_loop(0, 2, one_source, 0)


def far(head, ids, q, kv, acc, stat, *rest):
    return pl.pallas_call(
        functools.partial(far_kernel, head),
        out_shape=jax.ShapeDtypeStruct((4, 2, HD + 16, TOK), jnp.bfloat16),
        in_specs=[SM] + [VM] * (4 + len(rest)),
        out_specs=VM,
        input_output_aliases={5: 0} if rest else {},
        compiler_params=params(10),
    )(ids, q, kv, acc, stat, *rest)


def combine_kernel(parts_ref, out_ref):
    for h in range(2):
        lses = []
        for i in range(4):
            e = parts_ref[i, h, HD:HD + 16].astype(jnp.float32)
            lses.append(e[0:1] + e[1:2] + e[2:3])
        top = functools.reduce(jnp.maximum, lses)
        ws = [jnp.exp2(v - top) for v in lses]
        tot = ws[0] + ws[1] + ws[2] + ws[3]
        o = None
        for i in range(4):
            t = parts_ref[i, h, 0:HD].astype(jnp.float32) * (ws[i] / tot)
            o = t if o is None else o + t
        out_ref[:, h * HD:(h + 1) * HD] = o.T.astype(jnp.bfloat16)


def combine(parts):
    return pl.pallas_call(
        combine_kernel,
        out_shape=jax.ShapeDtypeStruct((TOK, 2 * HD), jnp.bfloat16),
        in_specs=[VM],
        out_specs=VM,
        compiler_params=params(10),
        name="combine",
    )(parts)


def spread(x, axis, n):
    many = jnp.broadcast_to(x[None], (n,) + x.shape)
    return lax.all_to_all(many, axis, 0, 0, tiled=True)


def body(stream, norm_gain, tile_vals, tile_row, tile_col, kept_count):
    zh = lax.axis_index("zh")
    core = lax.axis_index("core")
    plane = lax.axis_index(PLANE)
    block = zh * 16 + plane
    mine = lax.all_gather(stream, "zl", axis=0, tiled=False)
    tv = tile_vals[0]
    there = lax.ppermute(tv, "zh", [(0, 1), (1, 0)])
    near_tiles = spread(tv, PLANE, 16).reshape(-1, HD, HD)
    there_tiles = spread(there, PLANE, 16).reshape(-1, HD, HD)

    def order(v):
        v = v.reshape(2, 48)
        return jnp.where(zh == 0, v, v[::-1]).reshape(96)

    rows = order(tile_row[0])
    cols = order(tile_col[0])
    slot = order(jnp.arange(96, dtype=jnp.int32))
    live = (slot < kept_count[0]).astype(jnp.int32)
    half = HD // 2
    freq = jnp.exp(-math.log(rope_base) * jnp.arange(half, dtype=jnp.float32) / half)
    qpos = block * TOK + jnp.arange(TOK, dtype=jnp.int32)
    angles = qpos.astype(jnp.float32)[:, None] * freq[None, :]
    c = jnp.cos(angles)
    s = jnp.sin(angles)
    cosines = jnp.concatenate([c, c], axis=1)
    sines = jnp.concatenate([-s, s], axis=1)
    gain = norm_gain.reshape(16, 1, 512)
    mine, near_tiles, there_tiles, rows, cols, live, gain, cosines, sines = (
        lax.optimization_barrier(
            (mine, near_tiles, there_tiles, rows, cols, live, gain, cosines, sines)
        )
    )
    other = lax.ppermute(mine, "core", [(0, 1), (1, 0)])
    w = scatter(rows, cols, live, near_tiles, there_tiles)
    q, kv, kv0, kv1 = project(core.reshape(1), mine, other, w, gain, cosines, sines)
    across = [(b, 16 + b) for b in range(16)]
    far0 = lax.ppermute(kv0, CTX, across)
    far1 = lax.ppermute(kv1, CTX, across)
    keys = [kv]
    for k in range(1, 4):
        keys.append(lax.ppermute(kv, "y", [(y, y + k) for y in range(4 - k)]))
    q = lax.all_to_all(q, "x", 0, 0, tiled=True)
    far0 = spread(far0, "y", 4)
    far1 = spread(far1, "y", 4)
    ids = jnp.stack([zh, lax.axis_index("y"), lax.axis_index("x")]).astype(jnp.int32)
    acc, stat = near(ids, q, keys)
    out = far(0, ids, q, far0, acc, stat)
    out = far(1, ids, q, far1, acc, stat, out)
    return combine(lax.all_to_all(out, "x", 0, 0, tiled=True))


def solution(mesh):
    wide = Mesh(mesh.devices.reshape(2, 4, 4, 8, 2), CTX + HEAD)
    return jax.shard_map(
        body,
        mesh=wide,
        in_specs=(
            P(CTX, HEAD),
            P(),
            P(HEAD, CTX, None, None),
            P(HEAD, None),
            P(HEAD, None),
            P(HEAD),
        ),
        out_specs=P(CTX, HEAD),
        check_vma=False,
    )
```

```python
import functools
import math

import jax
import jax.numpy as jnp
from jax import lax
from jax.experimental import pallas as pl
from jax.experimental.pallas import tpu as pltpu
from jax.sharding import Mesh
from jax.sharding import PartitionSpec as P

D = 8192
HD = 128
TOK = 256
ROWS = D // HD
COLS = 6
PLANE = ("y", "x")
CTX = ("zh",) + PLANE
HEAD = ("zl", "core")
NEG = -1e30

rope_base = 1000000.0


VM = pl.BlockSpec(memory_space=pltpu.VMEM)
SM = pl.BlockSpec(memory_space=pltpu.SMEM)


def params(mib):
    return pltpu.CompilerParams(vmem_limit_bytes=mib * 1024 * 1024)


def line_at(i):
    return 2 * i if i < 4 else 15 - 2 * i


def scatter_kernel(row_ref, col_ref, live_ref, near_ref, there_ref, w_ref):
    def clear(i, c):
        w_ref[i] = jnp.zeros((HD, COLS * HD), jnp.bfloat16)
        return c

    lax.fori_loop(0, ROWS, clear, 0)
    half = near_ref.shape[0]
    for n, ref in enumerate((near_ref, there_ref)):

        def put(s, c, n=n, ref=ref):
            slot = n * half + s

            @pl.when(live_ref[slot] > 0)
            def _():
                at = pl.multiple_of(col_ref[slot] * HD, HD)
                w_ref[row_ref[slot], :, pl.ds(at, HD)] = ref[s]

            return c

        lax.fori_loop(0, half, put, 0)


def scatter(rows, cols, live, near_tiles, there_tiles):
    return pl.pallas_call(
        scatter_kernel,
        out_shape=jax.ShapeDtypeStruct((ROWS, HD, COLS * HD), jnp.bfloat16),
        in_specs=[SM, SM, SM, VM, VM],
        out_specs=VM,
        compiler_params=params(4),
        name="scatter_tiles",
    )(rows, cols, live, near_tiles, there_tiles)


def project_kernel(core_ref, mine_ref, other_ref, w_ref, gain_ref, cos_ref, sin_ref,
                   q_ref, kv_ref, kv0_ref, kv1_ref, acc_ref):
    core = core_ref[0]
    chunk = mine_ref.shape[2]
    per = chunk // HD

    def square(i, tot):
        for ref in (mine_ref, other_ref):
            for k in range(per):
                v = ref[i, :, k * HD:(k + 1) * HD].astype(jnp.float32)
                tot = tot + v * v
        return tot

    tot = lax.fori_loop(0, 8, square, jnp.zeros((TOK, HD), jnp.float32))
    r = lax.rsqrt(jnp.sum(tot, axis=1, keepdims=True) / D + 1e-05)
    acc_ref[...] = jnp.zeros_like(acc_ref)

    def step(i, c):
        at = jnp.where(i < 4, 2 * i, 15 - 2 * i)
        part = None
        for ref, cc in ((mine_ref, core), (other_ref, 1 - core)):
            x = ref[i].astype(jnp.float32) * r * gain_ref[2 * at + cc]
            w = w_ref[pl.ds((2 * at + cc) * per, per)].reshape(chunk, COLS * HD)
            d = jnp.dot(x.astype(jnp.bfloat16), w, preferred_element_type=jnp.float32)
            part = d if part is None else part + d
        acc_ref[...] += part
        return c

    lax.fori_loop(0, 8, step, 0, unroll=4)
    cosines = cos_ref[...]
    sines = sin_ref[...]

    def rot(v):
        return v * cosines + pltpu.roll(v, HD // 2, 1) * sines

    for h in range(2):
        q = rot(acc_ref[:, h * HD:(h + 1) * HD])
        k = rot(acc_ref[:, (2 + h) * HD:(3 + h) * HD]).astype(jnp.bfloat16)
        v = acc_ref[:, (4 + h) * HD:(5 + h) * HD]
        for half in range(2):
            at = slice(half * HD, (half + 1) * HD)
            qt = q[at].T.astype(jnp.bfloat16)
            for copy in range(4):
                q_ref[copy, 2 * h + half] = qt
            vt = v[at].T.astype(jnp.bfloat16)
            one = (kv0_ref, kv1_ref)[h]
            kv_ref[4 * h + half] = k[at]
            kv_ref[4 * h + 2 + half] = vt
            one[half] = k[at]
            one[2 + half] = vt


def project(core, mine, other, w, gain, cosines, sines):
    return pl.pallas_call(
        project_kernel,
        out_shape=(
            jax.ShapeDtypeStruct((4, 4, HD, HD), jnp.bfloat16),
            jax.ShapeDtypeStruct((8, HD, HD), jnp.bfloat16),
            jax.ShapeDtypeStruct((4, HD, HD), jnp.bfloat16),
            jax.ShapeDtypeStruct((4, HD, HD), jnp.bfloat16),
        ),
        in_specs=[SM] + [VM] * 6,
        out_specs=(VM,) * 4,
        scratch_shapes=[pltpu.VMEM((TOK, COLS * HD), jnp.float32)],
        compiler_params=params(10),
        name="project",
    )(core, mine, other, w, gain, cosines, sines)


SCALE = math.log2(math.e) / math.sqrt(HD)


def load_q(q_ref, n, h):
    return jnp.concatenate([q_ref[n, 2 * h], q_ref[n, 2 * h + 1]], axis=1)


def load_k(ref, h):
    return ref[2 * h * 2:2 * h * 2 + 2].reshape(TOK, HD)


def load_v(ref, h):
    return jnp.concatenate([ref[4 * h + 2], ref[4 * h + 3]], axis=1)


def near_kernel(ids_ref, q_ref, k0_ref, k1_ref, k2_ref, k3_ref, acc_ref, stat_ref):
    y = ids_ref[1]
    x = ids_ref[2]
    refs = (k0_ref, k1_ref, k2_ref, k3_ref)
    kids = [4 * lax.rem(y + 4 - k, 4) + x for k in range(4)]
    gap = lax.broadcasted_iota(jnp.int32, (TOK, TOK), 0) - lax.broadcasted_iota(
        jnp.int32, (TOK, TOK), 1
    )

    def one_source(n, c):
        qid = 4 * y + n
        for h in range(2):
            q = load_q(q_ref, n, h)
            ss = []
            for ref, kid in zip(refs, kids):
                s = jnp.dot(load_k(ref, h), q, preferred_element_type=jnp.float32)
                ss.append(jnp.where(gap <= (qid - kid) * TOK, s, NEG))
            top = functools.reduce(jnp.maximum, [jnp.max(s, axis=0, keepdims=True) for s in ss])
            acc = None
            total = None
            for ref, kid, s in zip(refs, kids, ss):
                p = jnp.where(gap <= (qid - kid) * TOK, jnp.exp2((s - top) * SCALE), 0.0)
                t = jnp.sum(p, axis=0, keepdims=True)
                o = jnp.dot(
                    load_v(ref, h), p.astype(jnp.bfloat16), preferred_element_type=jnp.float32
                )
                acc = o if acc is None else acc + o
                total = t if total is None else total + t
            acc_ref[2 * n + h] = acc
            stat_ref[2 * n + h, 0:1] = top
            stat_ref[2 * n + h, 1:2] = total
        return c

    lax.fori_loop(0, 4, one_source, 0)


STATE = (
    jax.ShapeDtypeStruct((8, HD, TOK), jnp.float32),
    jax.ShapeDtypeStruct((8, 8, TOK), jnp.float32),
)


def near(ids, q, keys):
    return pl.pallas_call(
        near_kernel,
        out_shape=STATE,
        in_specs=[SM] + [VM] * 5,
        out_specs=(VM, VM),
        compiler_params=params(10),
        name="attend_near",
    )(ids, q, *keys)


def fold(q_ref, refs, n, h, acc, old, total):
    q = load_q(q_ref, n, h)
    ss = [jnp.dot(load_k(ref, 0), q, preferred_element_type=jnp.float32) for ref in refs]
    top = functools.reduce(jnp.maximum, [jnp.max(s, axis=0, keepdims=True) for s in ss], old)
    fac = jnp.exp2((old - top) * SCALE)
    acc = acc * fac
    total = total * fac
    for s, ref in zip(ss, refs):
        p = jnp.exp2((s - top) * SCALE)
        total = total + jnp.sum(p, axis=0, keepdims=True)
        acc = acc + jnp.dot(
            load_v(ref, 0), p.astype(jnp.bfloat16), preferred_element_type=jnp.float32
        )
    return acc, top, total


def far_kernel(head, ids_ref, q_ref, kv_ref, acc_ref, stat_ref, *rest):
    out_ref = rest[-1]
    late = ids_ref[0] > 0

    def finish(n, acc, top, total):
        some = total > 0
        safe = jnp.where(some, total, 1.0)
        lse = jnp.where(some, top * SCALE + jnp.log2(safe), NEG)
        out_ref[n, head, 0:HD] = (acc / safe).astype(jnp.bfloat16)
        hi = lse.astype(jnp.bfloat16).astype(jnp.float32)
        mid = (lse - hi).astype(jnp.bfloat16).astype(jnp.float32)
        low = lse - hi - mid
        r = lax.broadcasted_iota(jnp.int32, (16, TOK), 0)
        extra = jnp.where(r == 0, hi, jnp.where(r == 1, mid, jnp.where(r == 2, low, 0.0)))
        out_ref[n, head, HD:HD + 16] = extra.astype(jnp.bfloat16)

    def state(n):
        i = 2 * n + head
        return acc_ref[i], stat_ref[i, 0:1], stat_ref[i, 1:2]

    @pl.when(jnp.logical_not(late))
    def _():
        for n in range(4):
            finish(n, *state(n))

    @pl.when(late)
    def _():
        def one_source(m, c):
            for n in (2 * m, 2 * m + 1):
                finish(n, *fold(q_ref, [kv_ref.at[k] for k in range(4)], n, head, *state(n)))
            return c

        lax.fori_loop(0, 2, one_source, 0)


def far(head, ids, q, kv, acc, stat, *rest):
    return pl.pallas_call(
        functools.partial(far_kernel, head),
        out_shape=jax.ShapeDtypeStruct((4, 2, HD + 16, TOK), jnp.bfloat16),
        in_specs=[SM] + [VM] * (4 + len(rest)),
        out_specs=VM,
        input_output_aliases={5: 0} if rest else {},
        compiler_params=params(10),
    )(ids, q, kv, acc, stat, *rest)


def combine_kernel(parts_ref, out_ref):
    for h in range(2):
        lses = []
        for i in range(4):
            e = parts_ref[i, h, HD:HD + 16].astype(jnp.float32)
            lses.append(e[0:1] + e[1:2] + e[2:3])
        top = functools.reduce(jnp.maximum, lses)
        ws = [jnp.exp2(v - top) for v in lses]
        tot = ws[0] + ws[1] + ws[2] + ws[3]
        o = None
        for i in range(4):
            t = parts_ref[i, h, 0:HD].astype(jnp.float32) * (ws[i] / tot)
            o = t if o is None else o + t
        out_ref[:, h * HD:(h + 1) * HD] = o.T.astype(jnp.bfloat16)


def combine(parts):
    return pl.pallas_call(
        combine_kernel,
        out_shape=jax.ShapeDtypeStruct((TOK, 2 * HD), jnp.bfloat16),
        in_specs=[VM],
        out_specs=VM,
        compiler_params=params(10),
        name="combine",
    )(parts)


def spread(x, axis, n):
    many = jnp.broadcast_to(x[None], (n,) + x.shape)
    return lax.all_to_all(many, axis, 0, 0, tiled=True)


def body(stream, norm_gain, tile_vals, tile_row, tile_col, kept_count):
    zh = lax.axis_index("zh")
    core = lax.axis_index("core")
    plane = lax.axis_index(PLANE)
    block = zh * 16 + plane
    mine = lax.all_gather(
        stream, "zl", axis=0, tiled=False, axis_index_groups=[[line_at(i) for i in range(8)]]
    )
    tv = tile_vals[0]
    there = lax.ppermute(tv, "zh", [(0, 1), (1, 0)])
    near_tiles = spread(tv, PLANE, 16).reshape(-1, HD, HD)
    there_tiles = spread(there, PLANE, 16).reshape(-1, HD, HD)

    def order(v):
        v = v.reshape(2, 48)
        return jnp.where(zh == 0, v, v[::-1]).reshape(96)

    rows = order(tile_row[0])
    cols = order(tile_col[0])
    slot = order(jnp.arange(96, dtype=jnp.int32))
    live = (slot < kept_count[0]).astype(jnp.int32)
    half = HD // 2
    freq = jnp.exp(-math.log(rope_base) * jnp.arange(half, dtype=jnp.float32) / half)
    qpos = block * TOK + jnp.arange(TOK, dtype=jnp.int32)
    angles = qpos.astype(jnp.float32)[:, None] * freq[None, :]
    c = jnp.cos(angles)
    s = jnp.sin(angles)
    cosines = jnp.concatenate([c, c], axis=1)
    sines = jnp.concatenate([-s, s], axis=1)
    gain = norm_gain.reshape(16, 1, 512)
    mine, near_tiles, there_tiles, rows, cols, live, gain, cosines, sines = (
        lax.optimization_barrier(
            (mine, near_tiles, there_tiles, rows, cols, live, gain, cosines, sines)
        )
    )
    other = lax.ppermute(mine, "core", [(0, 1), (1, 0)])
    w = scatter(rows, cols, live, near_tiles, there_tiles)
    q, kv, kv0, kv1 = project(core.reshape(1), mine, other, w, gain, cosines, sines)
    across = [(b, 16 + b) for b in range(16)]
    far0 = lax.ppermute(kv0, CTX, across)
    far1 = lax.ppermute(kv1, CTX, across)
    keys = [kv]
    for k in range(1, 4):
        keys.append(lax.ppermute(kv, "y", [(y, y + k) for y in range(4 - k)]))
    q = lax.all_to_all(q, "x", 0, 0, tiled=True)
    far0 = spread(far0, "y", 4)
    far1 = spread(far1, "y", 4)
    ids = jnp.stack([zh, lax.axis_index("y"), lax.axis_index("x")]).astype(jnp.int32)
    acc, stat = near(ids, q, keys)
    out = far(0, ids, q, far0, acc, stat)
    out = far(1, ids, q, far1, acc, stat, out)
    return combine(lax.all_to_all(out, "x", 0, 0, tiled=True))


def solution(mesh):
    wide = Mesh(mesh.devices.reshape(2, 4, 4, 8, 2), CTX + HEAD)
    return jax.shard_map(
        body,
        mesh=wide,
        in_specs=(
            P(CTX, HEAD),
            P(),
            P(HEAD, CTX, None, None),
            P(HEAD, None),
            P(HEAD, None),
            P(HEAD),
        ),
        out_specs=P(CTX, HEAD),
        check_vma=False,
    )
```

```python
import functools
import math

import jax
import jax.numpy as jnp
from jax import lax
from jax.experimental import pallas as pl
from jax.experimental.pallas import tpu as pltpu
from jax.sharding import Mesh
from jax.sharding import PartitionSpec as P

D = 8192
HD = 128
TOK = 256
ROWS = D // HD
COLS = 6
PLANE = ("y", "x")
CTX = ("zh",) + PLANE
HEAD = ("zl", "core")
NEG = -1e30

rope_base = 1000000.0


VM = pl.BlockSpec(memory_space=pltpu.VMEM)
SM = pl.BlockSpec(memory_space=pltpu.SMEM)


def params(mib):
    return pltpu.CompilerParams(vmem_limit_bytes=mib * 1024 * 1024)


def line_at(i):
    return 2 * i if i < 4 else 15 - 2 * i


def scatter_kernel(row_ref, col_ref, live_ref, near_ref, there_ref, w_ref):
    def clear(i, c):
        w_ref[i] = jnp.zeros((HD, COLS * HD), jnp.bfloat16)
        return c

    lax.fori_loop(0, ROWS, clear, 0)
    half = near_ref.shape[0]
    for n, ref in enumerate((near_ref, there_ref)):

        def put(s, c, n=n, ref=ref):
            slot = n * half + s

            @pl.when(live_ref[slot] > 0)
            def _():
                at = pl.multiple_of(col_ref[slot] * HD, HD)
                w_ref[row_ref[slot], :, pl.ds(at, HD)] = ref[s]

            return c

        lax.fori_loop(0, half, put, 0)


def scatter(rows, cols, live, near_tiles, there_tiles):
    return pl.pallas_call(
        scatter_kernel,
        out_shape=jax.ShapeDtypeStruct((ROWS, HD, COLS * HD), jnp.bfloat16),
        in_specs=[SM, SM, SM, VM, VM],
        out_specs=VM,
        compiler_params=params(4),
        name="scatter_tiles",
    )(rows, cols, live, near_tiles, there_tiles)


def project_kernel(core_ref, mine_ref, other_ref, w_ref, gain_ref, cos_ref, sin_ref,
                   q_ref, kv_ref, acc_ref):
    core = core_ref[0]
    chunk = mine_ref.shape[2]
    per = chunk // HD

    def square(i, tot):
        for ref in (mine_ref, other_ref):
            for k in range(per):
                v = ref[i, :, k * HD:(k + 1) * HD].astype(jnp.float32)
                tot = tot + v * v
        return tot

    tot = lax.fori_loop(0, 8, square, jnp.zeros((TOK, HD), jnp.float32))
    r = lax.rsqrt(jnp.sum(tot, axis=1, keepdims=True) / D + 1e-05)
    acc_ref[...] = jnp.zeros_like(acc_ref)

    def step(i, c):
        at = jnp.where(i < 4, 2 * i, 15 - 2 * i)
        part = None
        for ref, cc in ((mine_ref, core), (other_ref, 1 - core)):
            x = ref[i].astype(jnp.float32) * r * gain_ref[2 * at + cc]
            w = w_ref[pl.ds((2 * at + cc) * per, per)].reshape(chunk, COLS * HD)
            d = jnp.dot(x.astype(jnp.bfloat16), w, preferred_element_type=jnp.float32)
            part = d if part is None else part + d
        acc_ref[...] += part
        return c

    lax.fori_loop(0, 8, step, 0, unroll=4)
    cosines = cos_ref[...]
    sines = sin_ref[...]

    def rot(v):
        return v * cosines + pltpu.roll(v, HD // 2, 1) * sines

    for h in range(2):
        q = rot(acc_ref[:, h * HD:(h + 1) * HD])
        k = rot(acc_ref[:, (2 + h) * HD:(3 + h) * HD]).astype(jnp.bfloat16)
        v = acc_ref[:, (4 + h) * HD:(5 + h) * HD]
        for half in range(2):
            at = slice(half * HD, (half + 1) * HD)
            qt = q[at].T.astype(jnp.bfloat16)
            for copy in range(4):
                q_ref[copy, 2 * h + half] = qt
            vt = v[at].T.astype(jnp.bfloat16)
            kv_ref[4 * h + half] = k[at]
            kv_ref[4 * h + 2 + half] = vt


def project(core, mine, other, w, gain, cosines, sines):
    return pl.pallas_call(
        project_kernel,
        out_shape=(
            jax.ShapeDtypeStruct((4, 4, HD, HD), jnp.bfloat16),
            jax.ShapeDtypeStruct((8, HD, HD), jnp.bfloat16),
        ),
        in_specs=[SM] + [VM] * 6,
        out_specs=(VM, VM),
        scratch_shapes=[pltpu.VMEM((TOK, COLS * HD), jnp.float32)],
        compiler_params=params(10),
        name="project",
    )(core, mine, other, w, gain, cosines, sines)


SCALE = math.log2(math.e) / math.sqrt(HD)


def load_q(q_ref, n, h):
    return jnp.concatenate([q_ref[n, 2 * h], q_ref[n, 2 * h + 1]], axis=1)


def load_k(ref, h):
    return ref[2 * h * 2:2 * h * 2 + 2].reshape(TOK, HD)


def load_v(ref, h):
    return jnp.concatenate([ref[4 * h + 2], ref[4 * h + 3]], axis=1)


def near_kernel(ids_ref, q_ref, k0_ref, k1_ref, k2_ref, k3_ref, acc_ref, stat_ref):
    y = ids_ref[1]
    x = ids_ref[2]
    refs = (k0_ref, k1_ref, k2_ref, k3_ref)
    kids = [4 * lax.rem(y + 4 - k, 4) + x for k in range(4)]
    gap = lax.broadcasted_iota(jnp.int32, (TOK, TOK), 0) - lax.broadcasted_iota(
        jnp.int32, (TOK, TOK), 1
    )

    def one_source(n, c):
        qid = 4 * y + n
        for h in range(2):
            q = load_q(q_ref, n, h)
            ss = []
            for ref, kid in zip(refs, kids):
                s = jnp.dot(load_k(ref, h), q, preferred_element_type=jnp.float32)
                ss.append(jnp.where(gap <= (qid - kid) * TOK, s, NEG))
            top = functools.reduce(jnp.maximum, [jnp.max(s, axis=0, keepdims=True) for s in ss])
            acc = None
            total = None
            for ref, kid, s in zip(refs, kids, ss):
                p = jnp.where(gap <= (qid - kid) * TOK, jnp.exp2((s - top) * SCALE), 0.0)
                t = jnp.sum(p, axis=0, keepdims=True)
                o = jnp.dot(
                    load_v(ref, h), p.astype(jnp.bfloat16), preferred_element_type=jnp.float32
                )
                acc = o if acc is None else acc + o
                total = t if total is None else total + t
            acc_ref[2 * n + h] = acc
            stat_ref[2 * n + h, 0:1] = top
            stat_ref[2 * n + h, 1:2] = total
        return c

    lax.fori_loop(0, 4, one_source, 0)


STATE = (
    jax.ShapeDtypeStruct((8, HD, TOK), jnp.float32),
    jax.ShapeDtypeStruct((8, 8, TOK), jnp.float32),
)


def near(ids, q, keys):
    return pl.pallas_call(
        near_kernel,
        out_shape=STATE,
        in_specs=[SM] + [VM] * 5,
        out_specs=(VM, VM),
        compiler_params=params(10),
        name="attend_near",
    )(ids, q, *keys)


def fold(q_ref, refs, n, h, acc, old, total):
    q = load_q(q_ref, n, h)
    ss = [jnp.dot(load_k(ref, h), q, preferred_element_type=jnp.float32) for ref in refs]
    top = functools.reduce(jnp.maximum, [jnp.max(s, axis=0, keepdims=True) for s in ss], old)
    fac = jnp.exp2((old - top) * SCALE)
    acc = acc * fac
    total = total * fac
    for s, ref in zip(ss, refs):
        p = jnp.exp2((s - top) * SCALE)
        total = total + jnp.sum(p, axis=0, keepdims=True)
        acc = acc + jnp.dot(
            load_v(ref, h), p.astype(jnp.bfloat16), preferred_element_type=jnp.float32
        )
    return acc, top, total


def far_kernel(ids_ref, q_ref, k0_ref, k1_ref, acc_in, stat_in, acc_ref, stat_ref):
    late = ids_ref[0] > 0

    def one_source(n, c):
        for h in range(2):
            i = 2 * n + h
            acc = acc_in[i]
            top = stat_in[i, 0:1]
            total = stat_in[i, 1:2]
            acc, top, total = fold(q_ref, (k0_ref, k1_ref), n, h, acc, top, total)
            acc_ref[i] = acc
            stat_ref[i, 0:1] = top
            stat_ref[i, 1:2] = total
        return c

    @pl.when(late)
    def _():
        lax.fori_loop(0, 4, one_source, 0)

    @pl.when(jnp.logical_not(late))
    def _():
        acc_ref[...] = acc_in[...]
        stat_ref[...] = stat_in[...]


def far(ids, q, fars, acc, stat):
    return pl.pallas_call(
        far_kernel,
        out_shape=STATE,
        in_specs=[SM] + [VM] * 5,
        out_specs=(VM, VM),
        compiler_params=params(10),
        name="attend_far",
    )(ids, q, *fars, acc, stat)


def last_kernel(ids_ref, q_ref, k0_ref, k1_ref, acc_ref, stat_ref, out_ref):
    late = ids_ref[0] > 0

    def finish(n, h, acc, top, total):
        some = total > 0
        safe = jnp.where(some, total, 1.0)
        lse = jnp.where(some, top * SCALE + jnp.log2(safe), NEG)
        at = slice(h * TOK, (h + 1) * TOK)
        out_ref[n, 0:HD, at] = (acc / safe).astype(jnp.bfloat16)
        hi = lse.astype(jnp.bfloat16).astype(jnp.float32)
        mid = (lse - hi).astype(jnp.bfloat16).astype(jnp.float32)
        low = lse - hi - mid
        r = lax.broadcasted_iota(jnp.int32, (16, TOK), 0)
        extra = jnp.where(r == 0, hi, jnp.where(r == 1, mid, jnp.where(r == 2, low, 0.0)))
        out_ref[n, HD:HD + 16, at] = extra.astype(jnp.bfloat16)

    def state(n, h):
        i = 2 * n + h
        return acc_ref[i], stat_ref[i, 0:1], stat_ref[i, 1:2]

    @pl.when(jnp.logical_not(late))
    def _():
        def one_source(n, c):
            for h in range(2):
                finish(n, h, *state(n, h))
            return c

        lax.fori_loop(0, 4, one_source, 0)

    @pl.when(late)
    def _():
        def one_source(n, c):
            for h in range(2):
                finish(n, h, *fold(q_ref, (k0_ref, k1_ref), n, h, *state(n, h)))
            return c

        lax.fori_loop(0, 4, one_source, 0)


def last(ids, q, fars, acc, stat):
    return pl.pallas_call(
        last_kernel,
        out_shape=jax.ShapeDtypeStruct((4, HD + 16, 2 * TOK), jnp.bfloat16),
        in_specs=[SM] + [VM] * 5,
        out_specs=VM,
        compiler_params=params(10),
        name="attend_last",
    )(ids, q, *fars, acc, stat)


def combine_kernel(parts_ref, out_ref):
    count = parts_ref.shape[0]
    lses = []
    for i in range(count):
        e = parts_ref[i, HD:HD + 16].astype(jnp.float32)
        lses.append(e[0:1] + e[1:2] + e[2:3])
    top = functools.reduce(jnp.maximum, lses)
    ws = [jnp.exp2(v - top) for v in lses]
    tot = sum(ws)
    o = None
    for i in range(count):
        t = parts_ref[i, 0:HD].astype(jnp.float32) * (ws[i] / tot)
        o = t if o is None else o + t
    out_ref[:, :HD] = o[:, :TOK].T.astype(jnp.bfloat16)
    out_ref[:, HD:] = o[:, TOK:].T.astype(jnp.bfloat16)


def combine(parts):
    return pl.pallas_call(
        combine_kernel,
        out_shape=jax.ShapeDtypeStruct((TOK, 2 * HD), jnp.bfloat16),
        in_specs=[VM],
        out_specs=VM,
        compiler_params=params(10),
        name="combine",
    )(parts)


def spread(x, axis, n):
    many = jnp.broadcast_to(x[None], (n,) + x.shape)
    return lax.all_to_all(many, axis, 0, 0, tiled=True)


def body(stream, norm_gain, tile_vals, tile_row, tile_col, kept_count):
    zh = lax.axis_index("zh")
    core = lax.axis_index("core")
    plane = lax.axis_index(PLANE)
    block = zh * 16 + plane
    mine = lax.all_gather(
        stream, "zl", axis=0, tiled=False, axis_index_groups=[[line_at(i) for i in range(8)]]
    )
    tv = tile_vals[0]
    there = lax.ppermute(tv, "zh", [(0, 1), (1, 0)])
    near_tiles = spread(tv, PLANE, 16).reshape(-1, HD, HD)
    there_tiles = spread(there, PLANE, 16).reshape(-1, HD, HD)

    def order(v):
        v = v.reshape(2, 48)
        return jnp.where(zh == 0, v, v[::-1]).reshape(96)

    rows = order(tile_row[0])
    cols = order(tile_col[0])
    slot = order(jnp.arange(96, dtype=jnp.int32))
    live = (slot < kept_count[0]).astype(jnp.int32)
    half = HD // 2
    freq = jnp.exp(-math.log(rope_base) * jnp.arange(half, dtype=jnp.float32) / half)
    qpos = block * TOK + jnp.arange(TOK, dtype=jnp.int32)
    angles = qpos.astype(jnp.float32)[:, None] * freq[None, :]
    c = jnp.cos(angles)
    s = jnp.sin(angles)
    cosines = jnp.concatenate([c, c], axis=1)
    sines = jnp.concatenate([-s, s], axis=1)
    gain = norm_gain.reshape(16, 1, 512)
    mine, near_tiles, there_tiles, rows, cols, live, gain, cosines, sines = (
        lax.optimization_barrier(
            (mine, near_tiles, there_tiles, rows, cols, live, gain, cosines, sines)
        )
    )
    other = lax.ppermute(mine, "core", [(0, 1), (1, 0)])
    w = scatter(rows, cols, live, near_tiles, there_tiles)
    q, kv = project(core.reshape(1), mine, other, w, gain, cosines, sines)
    across = [(b, 16 + b) for b in range(16)]
    fars = [lax.ppermute(kv, CTX, across)]
    keys = [kv]
    for k in range(1, 4):
        keys.append(lax.ppermute(kv, "y", [(y, y + k) for y in range(4 - k)]))
    q = lax.all_to_all(q, "x", 0, 0, tiled=True)
    for k in (1, 3, 2):
        pairs = [
            (16 + 4 * y + x, 16 + 4 * ((y + k) % 4) + x) for y in range(4) for x in range(4)
        ]
        fars.append(lax.ppermute(fars[0], CTX, pairs))
    ids = jnp.stack([zh, lax.axis_index("y"), lax.axis_index("x")]).astype(jnp.int32)
    acc, stat = near(ids, q, keys)
    acc, stat = far(ids, q, fars[:2], acc, stat)
    out = last(ids, q, fars[2:], acc, stat)
    return combine(lax.all_to_all(out, "x", 0, 0, tiled=True))


def solution(mesh):
    wide = Mesh(mesh.devices.reshape(2, 4, 4, 8, 2), CTX + HEAD)
    return jax.shard_map(
        body,
        mesh=wide,
        in_specs=(
            P(CTX, HEAD),
            P(),
            P(HEAD, CTX, None, None),
            P(HEAD, None),
            P(HEAD, None),
            P(HEAD),
        ),
        out_specs=P(CTX, HEAD),
        check_vma=False,
    )
```

```python
import functools
import math

import jax
import jax.numpy as jnp
from jax import lax
from jax.experimental import pallas as pl
from jax.experimental.pallas import tpu as pltpu
from jax.sharding import Mesh
from jax.sharding import PartitionSpec as P

D = 8192
HD = 128
TOK = 256
ROWS = D // HD
COLS = 6
PLANE = ("y", "x")
CTX = ("zh",) + PLANE
HEAD = ("zl", "core")
NEG = -1e30

rope_base = 1000000.0


VM = pl.BlockSpec(memory_space=pltpu.VMEM)
SM = pl.BlockSpec(memory_space=pltpu.SMEM)


def params(mib):
    return pltpu.CompilerParams(vmem_limit_bytes=mib * 1024 * 1024)


def line_at(i):
    return 2 * i if i < 4 else 15 - 2 * i


def scatter_kernel(row_ref, col_ref, live_ref, near_ref, there_ref, w_ref):
    def clear(i, c):
        w_ref[i] = jnp.zeros((HD, COLS * HD), jnp.bfloat16)
        return c

    lax.fori_loop(0, ROWS, clear, 0)
    half = near_ref.shape[0]
    for n, ref in enumerate((near_ref, there_ref)):

        def put(s, c, n=n, ref=ref):
            slot = n * half + s

            @pl.when(live_ref[slot] > 0)
            def _():
                at = pl.multiple_of(col_ref[slot] * HD, HD)
                w_ref[row_ref[slot], :, pl.ds(at, HD)] = ref[s]

            return c

        lax.fori_loop(0, half, put, 0)


def scatter(rows, cols, live, near_tiles, there_tiles):
    return pl.pallas_call(
        scatter_kernel,
        out_shape=jax.ShapeDtypeStruct((ROWS, HD, COLS * HD), jnp.bfloat16),
        in_specs=[SM, SM, SM, VM, VM],
        out_specs=VM,
        compiler_params=params(4),
        name="scatter_tiles",
    )(rows, cols, live, near_tiles, there_tiles)


def project_kernel(core_ref, mine_ref, other_ref, w_ref, gain_ref, cos_ref, sin_ref,
                   q_ref, kv_ref, acc_ref):
    core = core_ref[0]
    chunk = mine_ref.shape[2]
    per = chunk // HD

    def square(i, tot):
        for ref in (mine_ref, other_ref):
            for k in range(per):
                v = ref[i, :, k * HD:(k + 1) * HD].astype(jnp.float32)
                tot = tot + v * v
        return tot

    tot = lax.fori_loop(0, 8, square, jnp.zeros((TOK, HD), jnp.float32))
    r = lax.rsqrt(jnp.sum(tot, axis=1, keepdims=True) / D + 1e-05)
    acc_ref[...] = jnp.zeros_like(acc_ref)

    def step(i, c):
        at = jnp.where(i < 4, 2 * i, 15 - 2 * i)
        part = None
        for ref, cc in ((mine_ref, core), (other_ref, 1 - core)):
            x = ref[i].astype(jnp.float32) * r * gain_ref[2 * at + cc]
            w = w_ref[pl.ds((2 * at + cc) * per, per)].reshape(chunk, COLS * HD)
            d = jnp.dot(x.astype(jnp.bfloat16), w, preferred_element_type=jnp.float32)
            part = d if part is None else part + d
        acc_ref[...] += part
        return c

    lax.fori_loop(0, 8, step, 0, unroll=8)
    cosines = cos_ref[...]
    sines = sin_ref[...]

    def rot(v):
        return v * cosines + pltpu.roll(v, HD // 2, 1) * sines

    for h in range(2):
        q = rot(acc_ref[:, h * HD:(h + 1) * HD]) * SCALE
        k = rot(acc_ref[:, (2 + h) * HD:(3 + h) * HD]).astype(jnp.bfloat16)
        v = acc_ref[:, (4 + h) * HD:(5 + h) * HD]
        for half in range(2):
            at = slice(half * HD, (half + 1) * HD)
            qt = q[at].T.astype(jnp.bfloat16)
            for copy in range(4):
                q_ref[copy, 2 * h + half] = qt
            vt = v[at].T.astype(jnp.bfloat16)
            kv_ref[4 * h + half] = k[at]
            kv_ref[4 * h + 2 + half] = vt


def project(core, mine, other, w, gain, cosines, sines):
    return pl.pallas_call(
        project_kernel,
        out_shape=(
            jax.ShapeDtypeStruct((4, 4, HD, HD), jnp.bfloat16),
            jax.ShapeDtypeStruct((8, HD, HD), jnp.bfloat16),
        ),
        in_specs=[SM] + [VM] * 6,
        out_specs=(VM, VM),
        scratch_shapes=[pltpu.VMEM((TOK, COLS * HD), jnp.float32)],
        compiler_params=params(10),
        name="project",
    )(core, mine, other, w, gain, cosines, sines)


SCALE = math.log2(math.e) / math.sqrt(HD)


def load_q(q_ref, n, h):
    return jnp.concatenate([q_ref[n, 2 * h], q_ref[n, 2 * h + 1]], axis=1)


def load_k(ref, h):
    return ref[2 * h * 2:2 * h * 2 + 2].reshape(TOK, HD)


def load_v(ref, h):
    return jnp.concatenate([ref[4 * h + 2], ref[4 * h + 3]], axis=1)


def near_kernel(ids_ref, q_ref, k0_ref, k1_ref, k2_ref, k3_ref, acc_ref, stat_ref):
    y = ids_ref[1]
    x = ids_ref[2]
    refs = (k0_ref, k1_ref, k2_ref, k3_ref)
    kids = [4 * lax.rem(y + 4 - k, 4) + x for k in range(4)]
    gap = lax.broadcasted_iota(jnp.int32, (TOK, TOK), 0) - lax.broadcasted_iota(
        jnp.int32, (TOK, TOK), 1
    )

    def one_source(n, c):
        qid = 4 * y + n
        for h in range(2):
            q = load_q(q_ref, n, h)
            ss = []
            for ref, kid in zip(refs, kids):
                s = jnp.dot(load_k(ref, h), q, preferred_element_type=jnp.float32)
                ss.append(jnp.where(gap <= (qid - kid) * TOK, s, NEG))
            top = functools.reduce(jnp.maximum, [jnp.max(s, axis=0, keepdims=True) for s in ss])
            acc = None
            total = None
            for ref, kid, s in zip(refs, kids, ss):
                p = jnp.where(gap <= (qid - kid) * TOK, jnp.exp2(s - top), 0.0)
                t = jnp.sum(p, axis=0, keepdims=True)
                o = jnp.dot(
                    load_v(ref, h), p.astype(jnp.bfloat16), preferred_element_type=jnp.float32
                )
                acc = o if acc is None else acc + o
                total = t if total is None else total + t
            acc_ref[2 * n + h] = acc
            stat_ref[2 * n + h, 0:1] = top
            stat_ref[2 * n + h, 1:2] = total
        return c

    lax.fori_loop(0, 4, one_source, 0, unroll=2)


STATE = (
    jax.ShapeDtypeStruct((8, HD, TOK), jnp.float32),
    jax.ShapeDtypeStruct((8, 8, TOK), jnp.float32),
)


def near(ids, q, keys):
    return pl.pallas_call(
        near_kernel,
        out_shape=STATE,
        in_specs=[SM] + [VM] * 5,
        out_specs=(VM, VM),
        compiler_params=params(10),
        name="attend_near",
    )(ids, q, *keys)


def fold(q_ref, refs, n, h, acc, old, total):
    q = load_q(q_ref, n, h)
    ss = [jnp.dot(load_k(ref, h), q, preferred_element_type=jnp.float32) for ref in refs]
    top = functools.reduce(jnp.maximum, [jnp.max(s, axis=0, keepdims=True) for s in ss], old)
    fac = jnp.exp2(old - top)
    acc = acc * fac
    total = total * fac
    for s, ref in zip(ss, refs):
        p = jnp.exp2(s - top)
        total = total + jnp.sum(p, axis=0, keepdims=True)
        acc = acc + jnp.dot(
            load_v(ref, h), p.astype(jnp.bfloat16), preferred_element_type=jnp.float32
        )
    return acc, top, total


def far_kernel(ids_ref, q_ref, k0_ref, k1_ref, acc_in, stat_in, acc_ref, stat_ref):
    late = ids_ref[0] > 0

    def one_source(n, c):
        for h in range(2):
            i = 2 * n + h
            acc = acc_in[i]
            top = stat_in[i, 0:1]
            total = stat_in[i, 1:2]
            acc, top, total = fold(q_ref, (k0_ref, k1_ref), n, h, acc, top, total)
            acc_ref[i] = acc
            stat_ref[i, 0:1] = top
            stat_ref[i, 1:2] = total
        return c

    @pl.when(late)
    def _():
        lax.fori_loop(0, 4, one_source, 0, unroll=2)

    @pl.when(jnp.logical_not(late))
    def _():
        acc_ref[...] = acc_in[...]
        stat_ref[...] = stat_in[...]


def far(ids, q, fars, acc, stat):
    return pl.pallas_call(
        far_kernel,
        out_shape=STATE,
        in_specs=[SM] + [VM] * 5,
        out_specs=(VM, VM),
        compiler_params=params(10),
        name="attend_far",
    )(ids, q, *fars, acc, stat)


def last_kernel(ids_ref, q_ref, k0_ref, k1_ref, acc_ref, stat_ref, out_ref):
    late = ids_ref[0] > 0

    def finish(n, h, acc, top, total):
        some = total > 0
        safe = jnp.where(some, total, 1.0)
        lse = jnp.where(some, top + jnp.log2(safe), NEG)
        at = slice(h * TOK, (h + 1) * TOK)
        out_ref[n, 0:HD, at] = (acc / safe).astype(jnp.bfloat16)
        hi = lse.astype(jnp.bfloat16).astype(jnp.float32)
        mid = (lse - hi).astype(jnp.bfloat16).astype(jnp.float32)
        low = lse - hi - mid
        r = lax.broadcasted_iota(jnp.int32, (16, TOK), 0)
        extra = jnp.where(r == 0, hi, jnp.where(r == 1, mid, jnp.where(r == 2, low, 0.0)))
        out_ref[n, HD:HD + 16, at] = extra.astype(jnp.bfloat16)

    def state(n, h):
        i = 2 * n + h
        return acc_ref[i], stat_ref[i, 0:1], stat_ref[i, 1:2]

    @pl.when(jnp.logical_not(late))
    def _():
        def one_source(n, c):
            for h in range(2):
                finish(n, h, *state(n, h))
            return c

        lax.fori_loop(0, 4, one_source, 0, unroll=2)

    @pl.when(late)
    def _():
        def one_source(n, c):
            for h in range(2):
                finish(n, h, *fold(q_ref, (k0_ref, k1_ref), n, h, *state(n, h)))
            return c

        lax.fori_loop(0, 4, one_source, 0, unroll=2)


def last(ids, q, fars, acc, stat):
    return pl.pallas_call(
        last_kernel,
        out_shape=jax.ShapeDtypeStruct((4, HD + 16, 2 * TOK), jnp.bfloat16),
        in_specs=[SM] + [VM] * 5,
        out_specs=VM,
        compiler_params=params(10),
        name="attend_last",
    )(ids, q, *fars, acc, stat)


def combine_kernel(parts_ref, out_ref):
    count = parts_ref.shape[0]
    lses = []
    for i in range(count):
        e = parts_ref[i, HD:HD + 16].astype(jnp.float32)
        lses.append(e[0:1] + e[1:2] + e[2:3])
    top = functools.reduce(jnp.maximum, lses)
    ws = [jnp.exp2(v - top) for v in lses]
    tot = sum(ws)
    o = None
    for i in range(count):
        t = parts_ref[i, 0:HD].astype(jnp.float32) * (ws[i] / tot)
        o = t if o is None else o + t
    out_ref[:, :HD] = o[:, :TOK].T.astype(jnp.bfloat16)
    out_ref[:, HD:] = o[:, TOK:].T.astype(jnp.bfloat16)


def combine(parts):
    return pl.pallas_call(
        combine_kernel,
        out_shape=jax.ShapeDtypeStruct((TOK, 2 * HD), jnp.bfloat16),
        in_specs=[VM],
        out_specs=VM,
        compiler_params=params(10),
        name="combine",
    )(parts)


def spread(x, axis, n):
    many = jnp.broadcast_to(x[None], (n,) + x.shape)
    return lax.all_to_all(many, axis, 0, 0, tiled=True)


def body(stream, norm_gain, tile_vals, tile_row, tile_col, kept_count):
    zh = lax.axis_index("zh")
    core = lax.axis_index("core")
    plane = lax.axis_index(PLANE)
    block = zh * 16 + plane
    mine = lax.all_gather(
        stream, "zl", axis=0, tiled=False, axis_index_groups=[[line_at(i) for i in range(8)]]
    )
    tv = tile_vals[0]
    there = lax.ppermute(tv, "zh", [(0, 1), (1, 0)])
    near_tiles = spread(tv, PLANE, 16).reshape(-1, HD, HD)
    there_tiles = spread(there, PLANE, 16).reshape(-1, HD, HD)

    def order(v):
        v = v.reshape(2, 48)
        return jnp.where(zh == 0, v, v[::-1]).reshape(96)

    rows = order(tile_row[0])
    cols = order(tile_col[0])
    slot = order(jnp.arange(96, dtype=jnp.int32))
    live = (slot < kept_count[0]).astype(jnp.int32)
    half = HD // 2
    freq = jnp.exp(-math.log(rope_base) * jnp.arange(half, dtype=jnp.float32) / half)
    qpos = block * TOK + jnp.arange(TOK, dtype=jnp.int32)
    angles = qpos.astype(jnp.float32)[:, None] * freq[None, :]
    c = jnp.cos(angles)
    s = jnp.sin(angles)
    cosines = jnp.concatenate([c, c], axis=1)
    sines = jnp.concatenate([-s, s], axis=1)
    gain = norm_gain.reshape(16, 1, 512)
    mine, near_tiles, there_tiles, rows, cols, live, gain, cosines, sines = (
        lax.optimization_barrier(
            (mine, near_tiles, there_tiles, rows, cols, live, gain, cosines, sines)
        )
    )
    other = lax.ppermute(mine, "core", [(0, 1), (1, 0)])
    w = scatter(rows, cols, live, near_tiles, there_tiles)
    q, kv = project(core.reshape(1), mine, other, w, gain, cosines, sines)
    across = [(b, 16 + b) for b in range(16)]
    fars = [lax.ppermute(kv, CTX, across)]
    keys = [kv]
    for k in range(1, 4):
        keys.append(lax.ppermute(kv, "y", [(y, y + k) for y in range(4 - k)]))
    q = lax.all_to_all(q, "x", 0, 0, tiled=True)
    for k in (1, 3, 2):
        pairs = [
            (16 + 4 * y + x, 16 + 4 * ((y + k) % 4) + x) for y in range(4) for x in range(4)
        ]
        fars.append(lax.ppermute(fars[0], CTX, pairs))
    ids = jnp.stack([zh, lax.axis_index("y"), lax.axis_index("x")]).astype(jnp.int32)
    acc, stat = near(ids, q, keys)
    acc, stat = far(ids, q, fars[:2], acc, stat)
    out = last(ids, q, fars[2:], acc, stat)
    return combine(lax.all_to_all(out, "x", 0, 0, tiled=True))


def solution(mesh):
    wide = Mesh(mesh.devices.reshape(2, 4, 4, 8, 2), CTX + HEAD)
    return jax.shard_map(
        body,
        mesh=wide,
        in_specs=(
            P(CTX, HEAD),
            P(),
            P(HEAD, CTX, None, None),
            P(HEAD, None),
            P(HEAD, None),
            P(HEAD),
        ),
        out_specs=P(CTX, HEAD),
        check_vma=False,
    )
```

```python
import functools
import math

import jax
import jax.numpy as jnp
from jax import lax
from jax.experimental import pallas as pl
from jax.experimental.pallas import tpu as pltpu
from jax.sharding import Mesh
from jax.sharding import PartitionSpec as P

D = 8192
HD = 128
TOK = 256
ROWS = D // HD
COLS = 6
PLANE = ("y", "x")
CTX = ("zh",) + PLANE
HEAD = ("zl", "core")
NEG = -1e30

rope_base = 1000000.0


VM = pl.BlockSpec(memory_space=pltpu.VMEM)
SM = pl.BlockSpec(memory_space=pltpu.SMEM)


def params(mib):
    return pltpu.CompilerParams(vmem_limit_bytes=mib * 1024 * 1024)


def line_at(i):
    return 2 * i if i < 4 else 15 - 2 * i


def scatter_kernel(row_ref, col_ref, live_ref, near_ref, there_ref, w_ref):
    def clear(i, c):
        w_ref[i] = jnp.zeros((HD, COLS * HD), jnp.bfloat16)
        return c

    lax.fori_loop(0, ROWS, clear, 0)
    half = near_ref.shape[0]
    for n, ref in enumerate((near_ref, there_ref)):

        def put(s, c, n=n, ref=ref):
            slot = n * half + s

            @pl.when(live_ref[slot] > 0)
            def _():
                at = pl.multiple_of(col_ref[slot] * HD, HD)
                w_ref[row_ref[slot], :, pl.ds(at, HD)] = ref[s]

            return c

        lax.fori_loop(0, half, put, 0)


def scatter(rows, cols, live, near_tiles, there_tiles):
    return pl.pallas_call(
        scatter_kernel,
        out_shape=jax.ShapeDtypeStruct((ROWS, HD, COLS * HD), jnp.bfloat16),
        in_specs=[SM, SM, SM, VM, VM],
        out_specs=VM,
        compiler_params=params(4),
        name="scatter_tiles",
    )(rows, cols, live, near_tiles, there_tiles)


def multiply(core, mine_ref, other_ref, w_ref, gain_ref, r, first, acc_ref):
    chunk = mine_ref.shape[2]
    per = chunk // HD
    width = acc_ref.shape[1]
    acc_ref[...] = jnp.zeros_like(acc_ref)

    def step(i, c):
        at = jnp.where(i < 4, 2 * i, 15 - 2 * i)
        part = None
        for ref, cc in ((mine_ref, core), (other_ref, 1 - core)):
            x = ref[i].astype(jnp.float32) * r * gain_ref[2 * at + cc]
            w = w_ref[pl.ds((2 * at + cc) * per, per), :, first:first + width]
            d = jnp.dot(
                x.astype(jnp.bfloat16),
                w.reshape(chunk, width),
                preferred_element_type=jnp.float32,
            )
            part = d if part is None else part + d
        acc_ref[...] += part
        return c

    lax.fori_loop(0, 8, step, 0, unroll=8)


def rot(v, cosines, sines):
    return v * cosines + pltpu.roll(v, HD // 2, 1) * sines


def keys_kernel(core_ref, mine_ref, other_ref, w_ref, gain_ref, cos_ref, sin_ref,
                kv_ref, r_ref, acc_ref):
    per = mine_ref.shape[2] // HD

    def square(i, tot):
        for ref in (mine_ref, other_ref):
            for k in range(per):
                v = ref[i, :, k * HD:(k + 1) * HD].astype(jnp.float32)
                tot = tot + v * v
        return tot

    tot = lax.fori_loop(0, 8, square, jnp.zeros((TOK, HD), jnp.float32))
    r = lax.rsqrt(jnp.sum(tot, axis=1, keepdims=True) / D + 1e-05)
    r_ref[...] = jnp.broadcast_to(r, (TOK, HD))
    multiply(core_ref[0], mine_ref, other_ref, w_ref, gain_ref, r, 2 * HD, acc_ref)
    for h in range(2):
        k = rot(acc_ref[:, h * HD:(h + 1) * HD], cos_ref[...], sin_ref[...])
        k = k.astype(jnp.bfloat16)
        v = acc_ref[:, (2 + h) * HD:(3 + h) * HD]
        for half in range(2):
            at = slice(half * HD, (half + 1) * HD)
            kv_ref[4 * h + half] = k[at]
            kv_ref[4 * h + 2 + half] = v[at].T.astype(jnp.bfloat16)


def queries_kernel(core_ref, mine_ref, other_ref, w_ref, gain_ref, cos_ref, sin_ref, r_ref,
                   q_ref, acc_ref):
    r = r_ref[:, 0:1]
    multiply(core_ref[0], mine_ref, other_ref, w_ref, gain_ref, r, 0, acc_ref)
    for h in range(2):
        q = rot(acc_ref[:, h * HD:(h + 1) * HD], cos_ref[...], sin_ref[...]) * SCALE
        for half in range(2):
            qt = q[half * HD:(half + 1) * HD].T.astype(jnp.bfloat16)
            for copy in range(4):
                q_ref[copy, 2 * h + half] = qt


def project_keys(*args):
    return pl.pallas_call(
        keys_kernel,
        out_shape=(
            jax.ShapeDtypeStruct((8, HD, HD), jnp.bfloat16),
            jax.ShapeDtypeStruct((TOK, HD), jnp.float32),
        ),
        in_specs=[SM] + [VM] * 6,
        out_specs=(VM, VM),
        scratch_shapes=[pltpu.VMEM((TOK, 4 * HD), jnp.float32)],
        compiler_params=params(10),
        name="project_keys",
    )(*args)


def project_queries(*args):
    return pl.pallas_call(
        queries_kernel,
        out_shape=jax.ShapeDtypeStruct((4, 4, HD, HD), jnp.bfloat16),
        in_specs=[SM] + [VM] * 7,
        out_specs=VM,
        scratch_shapes=[pltpu.VMEM((TOK, 2 * HD), jnp.float32)],
        compiler_params=params(10),
        name="project_queries",
    )(*args)


SCALE = math.log2(math.e) / math.sqrt(HD)


def load_q(q_ref, n, h):
    return jnp.concatenate([q_ref[n, 2 * h], q_ref[n, 2 * h + 1]], axis=1)


def load_k(ref, h):
    return ref[2 * h * 2:2 * h * 2 + 2].reshape(TOK, HD)


def load_v(ref, h):
    return jnp.concatenate([ref[4 * h + 2], ref[4 * h + 3]], axis=1)


def near_kernel(ids_ref, q_ref, k0_ref, k1_ref, k2_ref, k3_ref, acc_ref, stat_ref):
    y = ids_ref[1]
    x = ids_ref[2]
    refs = (k0_ref, k1_ref, k2_ref, k3_ref)
    kids = [4 * lax.rem(y + 4 - k, 4) + x for k in range(4)]
    gap = lax.broadcasted_iota(jnp.int32, (TOK, TOK), 0) - lax.broadcasted_iota(
        jnp.int32, (TOK, TOK), 1
    )

    def one_source(n, c):
        qid = 4 * y + n
        for h in range(2):
            q = load_q(q_ref, n, h)
            ss = []
            for ref, kid in zip(refs, kids):
                s = jnp.dot(load_k(ref, h), q, preferred_element_type=jnp.float32)
                ss.append(jnp.where(gap <= (qid - kid) * TOK, s, NEG))
            top = functools.reduce(jnp.maximum, [jnp.max(s, axis=0, keepdims=True) for s in ss])
            acc = None
            total = None
            for ref, kid, s in zip(refs, kids, ss):
                p = jnp.where(gap <= (qid - kid) * TOK, jnp.exp2(s - top), 0.0)
                t = jnp.sum(p, axis=0, keepdims=True)
                o = jnp.dot(
                    load_v(ref, h), p.astype(jnp.bfloat16), preferred_element_type=jnp.float32
                )
                acc = o if acc is None else acc + o
                total = t if total is None else total + t
            acc_ref[2 * n + h] = acc
            stat_ref[2 * n + h, 0:1] = top
            stat_ref[2 * n + h, 1:2] = total
        return c

    lax.fori_loop(0, 4, one_source, 0, unroll=2)


STATE = (
    jax.ShapeDtypeStruct((8, HD, TOK), jnp.float32),
    jax.ShapeDtypeStruct((8, 8, TOK), jnp.float32),
)


def near(ids, q, keys):
    return pl.pallas_call(
        near_kernel,
        out_shape=STATE,
        in_specs=[SM] + [VM] * 5,
        out_specs=(VM, VM),
        compiler_params=params(10),
        name="attend_near",
    )(ids, q, *keys)


def fold(q_ref, refs, n, h, acc, old, total):
    q = load_q(q_ref, n, h)
    ss = [jnp.dot(load_k(ref, h), q, preferred_element_type=jnp.float32) for ref in refs]
    top = functools.reduce(jnp.maximum, [jnp.max(s, axis=0, keepdims=True) for s in ss], old)
    fac = jnp.exp2(old - top)
    acc = acc * fac
    total = total * fac
    for s, ref in zip(ss, refs):
        p = jnp.exp2(s - top)
        total = total + jnp.sum(p, axis=0, keepdims=True)
        acc = acc + jnp.dot(
            load_v(ref, h), p.astype(jnp.bfloat16), preferred_element_type=jnp.float32
        )
    return acc, top, total


def far_kernel(ids_ref, q_ref, k0_ref, k1_ref, acc_in, stat_in, acc_ref, stat_ref):
    late = ids_ref[0] > 0

    def one_source(n, c):
        for h in range(2):
            i = 2 * n + h
            acc = acc_in[i]
            top = stat_in[i, 0:1]
            total = stat_in[i, 1:2]
            acc, top, total = fold(q_ref, (k0_ref, k1_ref), n, h, acc, top, total)
            acc_ref[i] = acc
            stat_ref[i, 0:1] = top
            stat_ref[i, 1:2] = total
        return c

    @pl.when(late)
    def _():
        lax.fori_loop(0, 4, one_source, 0, unroll=2)

    @pl.when(jnp.logical_not(late))
    def _():
        acc_ref[...] = acc_in[...]
        stat_ref[...] = stat_in[...]


def far(ids, q, fars, acc, stat):
    return pl.pallas_call(
        far_kernel,
        out_shape=STATE,
        in_specs=[SM] + [VM] * 5,
        out_specs=(VM, VM),
        compiler_params=params(10),
        name="attend_far",
    )(ids, q, *fars, acc, stat)


def last_kernel(ids_ref, q_ref, k0_ref, k1_ref, acc_ref, stat_ref, out_ref):
    late = ids_ref[0] > 0

    def finish(n, h, acc, top, total):
        some = total > 0
        safe = jnp.where(some, total, 1.0)
        lse = jnp.where(some, top + jnp.log2(safe), NEG)
        at = slice(h * TOK, (h + 1) * TOK)
        out_ref[n, 0:HD, at] = (acc / safe).astype(jnp.bfloat16)
        hi = lse.astype(jnp.bfloat16).astype(jnp.float32)
        mid = (lse - hi).astype(jnp.bfloat16).astype(jnp.float32)
        low = lse - hi - mid
        r = lax.broadcasted_iota(jnp.int32, (16, TOK), 0)
        extra = jnp.where(r == 0, hi, jnp.where(r == 1, mid, jnp.where(r == 2, low, 0.0)))
        out_ref[n, HD:HD + 16, at] = extra.astype(jnp.bfloat16)

    def state(n, h):
        i = 2 * n + h
        return acc_ref[i], stat_ref[i, 0:1], stat_ref[i, 1:2]

    @pl.when(jnp.logical_not(late))
    def _():
        def one_source(n, c):
            for h in range(2):
                finish(n, h, *state(n, h))
            return c

        lax.fori_loop(0, 4, one_source, 0, unroll=2)

    @pl.when(late)
    def _():
        def one_source(n, c):
            for h in range(2):
                finish(n, h, *fold(q_ref, (k0_ref, k1_ref), n, h, *state(n, h)))
            return c

        lax.fori_loop(0, 4, one_source, 0, unroll=2)


def last(ids, q, fars, acc, stat):
    return pl.pallas_call(
        last_kernel,
        out_shape=jax.ShapeDtypeStruct((4, HD + 16, 2 * TOK), jnp.bfloat16),
        in_specs=[SM] + [VM] * 5,
        out_specs=VM,
        compiler_params=params(10),
        name="attend_last",
    )(ids, q, *fars, acc, stat)


def combine_kernel(parts_ref, out_ref):
    count = parts_ref.shape[0]
    lses = []
    for i in range(count):
        e = parts_ref[i, HD:HD + 16].astype(jnp.float32)
        lses.append(e[0:1] + e[1:2] + e[2:3])
    top = functools.reduce(jnp.maximum, lses)
    ws = [jnp.exp2(v - top) for v in lses]
    tot = sum(ws)
    o = None
    for i in range(count):
        t = parts_ref[i, 0:HD].astype(jnp.float32) * (ws[i] / tot)
        o = t if o is None else o + t
    out_ref[:, :HD] = o[:, :TOK].T.astype(jnp.bfloat16)
    out_ref[:, HD:] = o[:, TOK:].T.astype(jnp.bfloat16)


def combine(parts):
    return pl.pallas_call(
        combine_kernel,
        out_shape=jax.ShapeDtypeStruct((TOK, 2 * HD), jnp.bfloat16),
        in_specs=[VM],
        out_specs=VM,
        compiler_params=params(10),
        name="combine",
    )(parts)


def spread(x, axis, n):
    many = jnp.broadcast_to(x[None], (n,) + x.shape)
    return lax.all_to_all(many, axis, 0, 0, tiled=True)


def body(stream, norm_gain, tile_vals, tile_row, tile_col, kept_count):
    zh = lax.axis_index("zh")
    core = lax.axis_index("core")
    plane = lax.axis_index(PLANE)
    block = zh * 16 + plane
    mine = lax.all_gather(
        stream, "zl", axis=0, tiled=False, axis_index_groups=[[line_at(i) for i in range(8)]]
    )
    tv = tile_vals[0]
    there = lax.ppermute(tv, "zh", [(0, 1), (1, 0)])
    near_tiles = spread(tv, PLANE, 16).reshape(-1, HD, HD)
    there_tiles = spread(there, PLANE, 16).reshape(-1, HD, HD)

    def order(v):
        v = v.reshape(2, 48)
        return jnp.where(zh == 0, v, v[::-1]).reshape(96)

    rows = order(tile_row[0])
    cols = order(tile_col[0])
    slot = order(jnp.arange(96, dtype=jnp.int32))
    live = (slot < kept_count[0]).astype(jnp.int32)
    half = HD // 2
    freq = jnp.exp(-math.log(rope_base) * jnp.arange(half, dtype=jnp.float32) / half)
    qpos = block * TOK + jnp.arange(TOK, dtype=jnp.int32)
    angles = qpos.astype(jnp.float32)[:, None] * freq[None, :]
    c = jnp.cos(angles)
    s = jnp.sin(angles)
    cosines = jnp.concatenate([c, c], axis=1)
    sines = jnp.concatenate([-s, s], axis=1)
    gain = norm_gain.reshape(16, 1, 512)
    mine, near_tiles, there_tiles, rows, cols, live, gain, cosines, sines = (
        lax.optimization_barrier(
            (mine, near_tiles, there_tiles, rows, cols, live, gain, cosines, sines)
        )
    )
    other = lax.ppermute(mine, "core", [(0, 1), (1, 0)])
    w = scatter(rows, cols, live, near_tiles, there_tiles)
    parts = (core.reshape(1), mine, other, w, gain, cosines, sines)
    kv, r = project_keys(*parts)
    across = [(b, 16 + b) for b in range(16)]
    fars = [lax.ppermute(kv, CTX, across)]
    keys = [kv]
    for k in range(1, 4):
        keys.append(lax.ppermute(kv, "y", [(y, y + k) for y in range(4 - k)]))
    q = project_queries(*parts, r)
    q = lax.all_to_all(q, "x", 0, 0, tiled=True)
    for k in (1, 3, 2):
        pairs = [
            (16 + 4 * y + x, 16 + 4 * ((y + k) % 4) + x) for y in range(4) for x in range(4)
        ]
        fars.append(lax.ppermute(fars[0], CTX, pairs))
    ids = jnp.stack([zh, lax.axis_index("y"), lax.axis_index("x")]).astype(jnp.int32)
    acc, stat = near(ids, q, keys)
    acc, stat = far(ids, q, fars[:2], acc, stat)
    out = last(ids, q, fars[2:], acc, stat)
    return combine(lax.all_to_all(out, "x", 0, 0, tiled=True))


def solution(mesh):
    wide = Mesh(mesh.devices.reshape(2, 4, 4, 8, 2), CTX + HEAD)
    return jax.shard_map(
        body,
        mesh=wide,
        in_specs=(
            P(CTX, HEAD),
            P(),
            P(HEAD, CTX, None, None),
            P(HEAD, None),
            P(HEAD, None),
            P(HEAD),
        ),
        out_specs=P(CTX, HEAD),
        check_vma=False,
    )
```
